512 devices in a mesh: depth: 16 (over x_hi, z), height: 32 (over x_lo, y, core).
Axes of the slice: x: 4 (x_hi: 2, x_lo: 2; x = x_hi * 2 + x_lo), y: 8, z: 8, core: 2. Of those that a mesh axis runs over, the one named last changes fastest.
Arguments:
- grad_out: bfloat16 [16, 64, 64, 1024], P('depth', 'height'), may hold values from -6 to 6
- pre_act: bfloat16 [16, 64, 64, 1024], P('depth', None, None, 'height'), may hold values from -6 to 6
- w_in: bfloat16 [1024, 1024], P('depth'), may hold values from -0.1875 to 0.1875
- w_out: bfloat16 [1024, 1024], P('depth'), may hold values from -0.1875 to 0.1875
- kernel: bfloat16 [27, 32, 1024], P(None, None, 'height'), may hold values from -0.21875 to 0.21875
Outputs:
- grad_in: bfloat16 [16, 64, 64, 1024], P('depth', 'height')
- kernel_grad: float32 [27, 32, 1024], P(None, None, 'height')
The draws below stay inside these ranges and needn't reach their ends.
All inputs are finite; a program needn't handle non-finite values.
Results may differ from the reference program's by a relative error of at most 0.014.
Values may be sent and summed in bfloat16 or wider, within the bound.
A program may use at most 64 MiB of HBM per device.

```python
import jax
import jax.numpy as jnp
from jax import lax

C = 1024
CG = 32
WID = 64
DT = 16
HT = 64
CELLS = 65536


def block_scale(own_key, extent, shards, smallest, top_value):
    factor_of, own = 1.0, jax.random.fold_in(own_key, 6)
    for dim, blocks in shards:
        steps = jnp.exp(jax.random.uniform(jax.random.fold_in(own, dim), (blocks,), jnp.float32, smallest / len(shards), top_value / len(shards)))
        factor_of = factor_of * jnp.repeat(steps, extent[dim] // blocks).reshape([-1 if axis == dim else 1 for axis in range(len(extent))])
    return factor_of


def normal_values(key, shape, scale, bound, split=(), dtype=jnp.bfloat16):
    result = scale * jax.random.normal(key, shape, jnp.float32)
    if split:
        result = result * block_scale(key, shape, split, -0.22, 0.18)
    return jnp.clip(result, -bound, bound).astype(dtype)


def setup_inputs(seed: int = 0) -> dict:
    splits = jax.random.split(jax.random.key(seed), 6)
    grad_out = normal_values(splits[0], (DT, HT, WID, C), 1.0, 6.0, ((0, 16), (1, 32)))
    pre_act = normal_values(splits[1], (DT, HT, WID, C), 1.0, 6.0, ((0, 16), (3, 32)))
    w_in = normal_values(splits[2], (C, C), C ** -0.5, 0.1875, ((0, 16),))
    w_out = normal_values(splits[3], (C, C), C ** -0.5, 0.1875, ((0, 16),))
    kernel = normal_values(splits[4], (27, CG, C), (27 * CG) ** -0.5, 0.21875, ((2, 32),))
    return dict(grad_out=grad_out, pre_act=pre_act, w_in=w_in, w_out=w_out, kernel=kernel)


def reference(grad_out, pre_act, w_in, w_out, kernel):
    depth_len, height_len, width_len, chans = grad_out.shape
    group_width = kernel.shape[1]
    group_count = chans // group_width
    flat = grad_out.reshape(-1, chans)
    grad_mid = jnp.dot(flat, w_out.T, preferred_element_type=jnp.float32).astype(jnp.bfloat16)
    grad_mid = grad_mid.reshape(depth_len, height_len, width_len, group_count, group_width)
    moved = jnp.moveaxis(grad_mid, 3, 0)
    pre_groups = jnp.moveaxis(pre_act.reshape(depth_len, height_len, width_len, group_count, group_width), 3, 0)
    kern = jnp.transpose(kernel.reshape(27, group_width, group_count, group_width), (2, 0, 1, 3))

    def per_group(items):
        mid, pre, weights = items
        hidden = jnp.maximum(pre, 0).astype(jnp.float32)
        padded = jnp.pad(mid.astype(jnp.float32), ((1, 1), (1, 1), (1, 1), (0, 0)))
        back = jnp.zeros(hidden.shape, jnp.float32)
        grads = []
        for step_d in (-1, 0, 1):
            for step_h in (-1, 0, 1):
                for step_w in (-1, 0, 1):
                    index = 9 * (step_d + 1) + 3 * (step_h + 1) + (step_w + 1)
                    window = padded[1 - step_d:1 - step_d + depth_len, 1 - step_h:1 - step_h + height_len, 1 - step_w:1 - step_w + width_len, :]
                    back = back + jnp.einsum('dhwo,io->dhwi', window, weights[index].astype(jnp.float32))
                    grads.append(jnp.einsum('dhwo,dhwi->io', window, hidden))
        masked = jnp.where(pre > 0, back, jnp.zeros_like(back)).astype(jnp.bfloat16)
        return masked, jnp.stack(grads)

    masked, kgrads = lax.map(per_group, (moved, pre_groups, kern))
    grad_pre = jnp.moveaxis(masked, 0, 3).reshape(depth_len, height_len, width_len, chans)
    scale = jnp.float32(CELLS) ** -0.5
    kernel_grad = jnp.transpose(kgrads, (1, 2, 0, 3)).reshape(27, group_width, chans) * scale
    branch = jnp.dot(grad_pre.reshape(-1, chans), w_in.T, preferred_element_type=jnp.float32)
    grad_in = (grad_out.astype(jnp.float32) + branch.reshape(grad_out.shape)).astype(jnp.bfloat16)
    return grad_in, kernel_grad
```

```python
import functools

import jax
import jax.numpy as jnp
from jax import lax
from jax.experimental import pallas as pl
from jax.experimental.pallas import tpu as pltpu
from jax.sharding import PartitionSpec as P

MESH = pl.DeviceIdType.MESH
BF = jnp.bfloat16
F32 = jnp.float32


def body(
    DN, C,
    go_ref, pre_ref, wi_ref, wo_ref, kern_ref,
    out_ref, kg_ref,
    go_buf, wo_buf, wi_buf, wi_own, mt_buf, m_buf, xa, xb, pre2, kmf, kmat, acc, gp_stage, gpr,
    gbuf, g_stage, g_recv, g_fin, p_send, p_recv,
    go_sem, wo_s, wo_r, wi_s, wi_r, a1_s, a1_r, h_s, h_r, a2_s, a2_r, rs_s, rs_r, ag_s, ag_r, p_s, p_r,
):
    HN = 2 * DN
    Z = DN // 2
    HALF = Z // 2
    NQ = HN // 4
    NCH = h_s.shape[1]
    KPC = DN // NCH
    SPD = g_stage.shape[1]
    NP = p_send.shape[0]
    PW = C // NP

    d = lax.axis_index("depth")
    h = lax.axis_index("height")
    k = h // 2
    c = h % 2
    xh = d // Z
    z = d % Z

    def remote(src, dst, ss, rs, dd, hh):
        return pltpu.make_async_remote_copy(
            src_ref=src, dst_ref=dst, send_sem=ss, recv_sem=rs, device_id=(dd, hh), device_id_type=MESH
        )

    partner = 2 * k + (1 - c)

    barrier = pltpu.get_barrier_semaphore()
    pl.semaphore_signal(barrier, inc=1, device_id=(d, partner), device_id_type=MESH)

    @pl.loop(1, DN)
    def _(j):
        pl.semaphore_signal(barrier, inc=1, device_id=((d + j) % DN, h), device_id_type=MESH)
        pl.semaphore_signal(barrier, inc=1, device_id=(d, 2 * ((k + j) % DN) + c), device_id_type=MESH)

    zero_tile = jnp.zeros((32, 128), BF)
    for s in range(3):
        m_buf[s, 0] = zero_tile
        m_buf[s, HN + 1] = zero_tile

    @pl.when(d == 0)
    def _():
        m_buf[2] = jnp.zeros(m_buf.shape[1:], BF)

    @pl.when(d == DN - 1)
    def _():
        m_buf[0] = jnp.zeros(m_buf.shape[1:], BF)

    go_buf[pl.ds(pl.multiple_of(128 * c, 128), 128), :] = go_ref[...]

    for o in range(27):
        s, m = divmod(o, 9)
        kmf[s, :, 32 * m : 32 * m + 32] = kern_ref[o].astype(F32)
    for s in range(3):
        kmat[s] = kmf[s].astype(BF)

    @pl.loop(0, HN)
    def _(t):
        both = jnp.concatenate([pre_ref[2 * t].astype(F32), pre_ref[2 * t + 1].astype(F32)], axis=1)
        pre2[t] = both.astype(BF)

    col = lax.broadcasted_iota(jnp.int32, (C, C // 2), 1)
    row = lax.broadcasted_iota(jnp.int32, (C, C // 2), 0)
    pick = jnp.where(row == 64 * (col // 32) + 32 * c + col % 32, 1.0, 0.0).astype(BF)
    wi_own[...] = jnp.dot(wi_ref[...], pick, preferred_element_type=F32).astype(BF)

    pl.semaphore_wait(barrier, 1 + 2 * (DN - 1))

    go_copy = remote(
        go_ref, go_buf.at[pl.ds(pl.multiple_of(128 * c, 128), 128), :], go_sem.at[0], go_sem.at[1], d, partner
    )
    go_copy.start()

    class Ring:
        def __init__(self, own, buf, ss, rs):
            self.own, self.buf, self.ss, self.rs = own, buf, ss, rs
            self.sent = []

        def idx(self, far, dz):
            side = 1 - xh if far else xh
            return side * Z + (z + dz + Z) % Z

        def send(self, far, dz, step):
            i = self.idx(far, dz)
            src = self.own if (not far and dz == 0) else self.buf.at[i]
            copy = remote(
                src, self.buf.at[i], self.ss.at[len(self.sent)], self.rs.at[i], xh * Z + (z + step + Z) % Z, h
            )
            copy.start()
            self.sent.append(copy)

        def begin(self):
            if HALF >= 1:
                self.send(False, 0, 1)
            copy = remote(
                self.own, self.buf.at[d], self.ss.at[len(self.sent)], self.rs.at[d], (1 - xh) * Z + z, h
            )
            copy.start()
            self.sent.append(copy)
            if HALF - 1 >= 1:
                self.send(False, 0, -1)

        def take(self, far, dz):
            i = self.idx(far, dz)
            remote(self.buf.at[i], self.buf.at[i], self.ss.at[0], self.rs.at[i], d, partner).wait_recv()
            return i

        def arrivals(self, s):
            if s == 0:
                return [(True, 0, 0)]
            out = []
            if s <= HALF:
                out.append((False, -s, 1))
            if s <= HALF:
                out.append((True, s, -1))
            if s <= HALF - 1:
                out.append((False, s, -1))
                out.append((True, -s, 1))
            return out

        def pump(self, s, work=None):
            for far, dz, step in self.arrivals(s):
                i = self.take(far, dz)
                if s == 0:
                    if HALF >= 1:
                        self.send(True, 0, -1)
                    if HALF - 1 >= 1:
                        self.send(True, 0, 1)
                else:
                    limit = HALF if (far == (step < 0)) else HALF - 1
                    if s + 1 <= limit:
                        self.send(far, dz, step)
                if work is not None:
                    work(i)

        def finish(self):
            for copy in self.sent:
                copy.wait_send()

    own_rows = wo_ref.at[pl.ds(pl.multiple_of(32 * c, 32), 32), :]
    ring_o = Ring(own_rows, wo_buf, wo_s, wo_r)
    ring_i = Ring(wi_own, wi_buf, wi_s, wi_r)
    ring_o.begin()

    def project(block, i):
        mid = lax.dot_general(block, go_buf[...], (((1,), (1,)), ((), ())), preferred_element_type=F32)
        mid = mid.astype(BF)

        @pl.when(i == k)
        def _():
            m_buf[1, 1 + 2 * i] = mid[:, :128]
            m_buf[1, 2 + 2 * i] = mid[:, 128:]

        @pl.when(i != k)
        def _():
            mt_buf[i, 0] = mid[:, :128]
            mt_buf[i, 1] = mid[:, 128:]
            remote(
                mt_buf.at[i], m_buf.at[1, pl.ds(1 + 2 * k, 2)], a1_s.at[i], a1_r.at[k], d, 2 * i + c
            ).start()

    go_copy.wait_recv()
    project(own_rows[...], d)
    for s in range(HALF + 1):
        ring_o.pump(s, lambda i: project(wo_buf[i], i))

    up, down = jnp.minimum(d + 1, DN - 1), jnp.maximum(d - 1, 0)

    def halo(n, side):
        part = pl.ds(1 + 2 * KPC * n, 2 * KPC)
        return remote(
            m_buf.at[1, part],
            m_buf.at[2 if side == 0 else 0, part],
            h_s.at[side, n],
            h_r.at[side, n],
            up if side == 0 else down,
            h,
        )

    for n in range(NCH):
        for j in range(KPC):
            i = KPC * n + j

            @pl.when(i != k)
            def _(i=i):
                part = m_buf.at[1, pl.ds(1 + 2 * i, 2)]
                remote(part, part, a1_s.at[0], a1_r.at[i], d, partner).wait_recv()

        @pl.when(d < DN - 1)
        def _(n=n):
            halo(n, 0).start()

        @pl.when(d > 0)
        def _(n=n):
            halo(n, 1).start()

    ring_i.begin()

    lane = lax.broadcasted_iota(jnp.int32, (4, 32, 128), 2)
    low = lane < 64
    first = lane % 64 == 0
    last = lane % 64 == 63

    def widen(dst, s, at, n, v):
        v0 = v[:n]
        zero = jnp.zeros_like(v0)
        dst[s, pl.ds(at, n), 0:32, :] = jnp.where(last[:n], zero, pltpu.roll(v0, 127, 2)).astype(BF)
        dst[s, pl.ds(at, n), 32:64, :] = v0.astype(BF)
        dst[s, pl.ds(at, n), 64:96, :] = jnp.where(first[:n], zero, pltpu.roll(v0, 1, 2)).astype(BF)

    def spread(s):
        @pl.loop(0, NQ)
        def _(q):
            here = m_buf[s, pl.ds(1 + 4 * q, 4)].astype(F32)
            before = m_buf[s, pl.ds(4 * q, 4)].astype(F32)
            widen(xa, s, 4 * q, 4, here)
            widen(xb, s, 4 * q, 4, jnp.where(low, pltpu.roll(before, 64, 2), pltpu.roll(here, 64, 2)))

        end = m_buf[s, pl.ds(HN, 1)].astype(F32)
        widen(xb, s, HN, 1, jnp.where(low[:1], pltpu.roll(end, 64, 2), jnp.zeros_like(end)))

    def columns(s, q):
        tiles = []
        for j in range(4):
            t = 4 * q + j
            tiles.append(jnp.concatenate([xb[s, t + 1], xa[s, t], xb[s, t]], axis=0))
        return jnp.concatenate(tiles, axis=1)

    def hidden(q):
        tiles = [jnp.maximum(pre2[4 * q + j], jnp.zeros((32, 128), BF)) for j in range(4)]
        return jnp.concatenate(tiles, axis=1)

    def outer(x, q):
        return lax.dot_general(hidden(q), x, (((1,), (1,)), ((), ())), preferred_element_type=F32)

    gbuf[...] = jnp.zeros_like(gbuf)

    spread(1)

    @pl.loop(0, NQ)
    def _(q):
        x = columns(1, q)
        acc[q] = jnp.dot(kmat[1], x, preferred_element_type=F32)
        gbuf[1, :, 0:288] += outer(x, q)

    ring_i.pump(0)
    ring_i.pump(1)

    for n in range(NCH):
        @pl.when(d < DN - 1)
        def _(n=n):
            halo(n, 1).wait_recv()

        @pl.when(d > 0)
        def _(n=n):
            halo(n, 0).wait_recv()

    spread(0)
    spread(2)
    if HALF >= 2:
        ring_i.pump(2)

    @pl.loop(0, NQ)
    def _(p):
        q = (p + k // 2) % NQ
        back = acc[q] + jnp.dot(kmat[0], columns(0, q), preferred_element_type=F32)
        back = back + jnp.dot(kmat[2], columns(2, q), preferred_element_type=F32)
        for j in range(4):
            gate = pre2[4 * q + j].astype(F32) > 0
            tile = jnp.where(gate, back[:, 128 * j : 128 * j + 128], jnp.zeros((32, 128), F32))
            gp_stage[4 * q + j] = tile.astype(BF)
        for j in range(2):
            i = 2 * q + j

            @pl.when(i == k)
            def _(i=i):
                for t in range(2):
                    gpr[t, pl.ds(pl.multiple_of(32 * k, 32), 32), :] = gp_stage[2 * i + t]

            @pl.when(i != k)
            def _(i=i):
                remote(
                    gp_stage.at[pl.ds(2 * i, 2)],
                    gpr.at[:, pl.ds(pl.multiple_of(32 * k, 32), 32), :],
                    a2_s.at[i],
                    a2_r.at[k],
                    d,
                    2 * i + c,
                ).start()

    if HALF >= 3:
        ring_i.pump(3)

    @pl.loop(0, NQ)
    def _(q):
        gbuf[0, :, 0:288] += outer(columns(0, q), q)
        gbuf[2, :, 0:288] += outer(columns(2, q), q)

    def slot(f):
        return f // SPD, f % SPD

    def cut(f):
        s, rest = divmod(f, 12)
        rb, lt = divmod(rest, 3)
        return s, slice(8 * rb, 8 * rb + 8), slice(128 * lt, 128 * lt + 128)

    for f in range(SPD * DN):
        a, b = slot(f)
        g_stage[a, b] = gbuf[cut(f)].astype(BF) if f < 36 else jnp.zeros((8, 128), BF)

    @pl.loop(1, DN)
    def _(j):
        r = (d + j) % DN
        remote(g_stage.at[r], g_recv.at[d], rs_s.at[r], rs_r.at[d], r, h).start()

    for s in range(4, HALF + 1):
        ring_i.pump(s)
    wi_buf[d] = wi_own[...]

    @pl.loop(1, DN)
    def _(j):
        i = (k + j) % DN
        part = gpr.at[:, pl.ds(pl.multiple_of(32 * i, 32), 32), :]
        remote(part, part, a2_s.at[0], a2_r.at[i], d, partner).wait_recv()

    rows_p = wi_buf.shape[0] // NP

    def half(cells, n):
        w = wi_buf[rows_p * n : rows_p * (n + 1)].reshape(PW, C // 2)
        return lax.dot_general(cells, w, (((1,), (1,)), ((), ())), preferred_element_type=F32)

    theirs = gpr[1 - c].T
    exchange = []
    for n in range(NP):
        p_send[n] = half(theirs, n)
        copy = remote(p_send.at[n], p_recv.at[n], p_s.at[n], p_r.at[n], d, partner)
        copy.start()
        exchange.append(copy)

    total = g_stage[d].astype(F32)
    for j in range(1, DN):
        r = (d + j) % DN
        remote(g_recv.at[r], g_recv.at[r], rs_s.at[0], rs_r.at[r], d, partner).wait_recv()
        total = total + g_recv[r].astype(F32)
    g_fin[d] = total.astype(BF)

    @pl.loop(1, DN)
    def _(j):
        r = (d + j) % DN
        remote(g_fin.at[d], g_fin.at[d], ag_s.at[r], ag_r.at[d], r, h).start()

    mine = gpr[c].T
    for n in range(NP):
        part = half(mine, n)
        exchange[n].wait_recv()
        cols = slice(PW * n, PW * (n + 1))
        out_ref[:, cols] = (go_ref[:, cols].astype(F32) + (part + p_recv[n])).astype(BF)

    @pl.loop(1, DN)
    def _(j):
        r = (d + j) % DN
        remote(g_fin.at[r], g_fin.at[r], ag_s.at[0], ag_r.at[r], d, partner).wait_recv()

    scale = float(DN * 2 * HN * 64) ** -0.5
    for f in range(36):
        gbuf[cut(f)] = g_fin[slot(f)].astype(F32) * scale
    for o in range(27):
        s, m = divmod(o, 9)
        kg_ref[o] = gbuf[s, :, 32 * m : 32 * m + 32]

    go_copy.wait_send()
    ring_o.finish()
    ring_i.finish()
    for copy in exchange:
        copy.wait_send()
    for n in range(NCH):
        @pl.when(d < DN - 1)
        def _(n=n):
            halo(n, 0).wait_send()

        @pl.when(d > 0)
        def _(n=n):
            halo(n, 1).wait_send()

    @pl.loop(1, DN)
    def _(j):
        i = (k + j) % DN
        r = (d + j) % DN
        remote(mt_buf.at[i], mt_buf.at[i], a1_s.at[i], a1_r.at[i], d, partner).wait_send()
        part = gp_stage.at[pl.ds(2 * i, 2)]
        remote(part, part, a2_s.at[i], a2_r.at[i], d, partner).wait_send()
        remote(g_stage.at[r], g_recv.at[r], rs_s.at[r], rs_r.at[r], d, partner).wait_send()
        remote(g_fin.at[d], g_fin.at[d], ag_s.at[r], ag_r.at[r], d, partner).wait_send()


def shards(DN, grad_out, pre_act, w_in, w_out, kernel):
    C = grad_out.shape[-1]
    HN = 2 * DN
    rows = grad_out.reshape(128, C)
    turned = jnp.transpose(pre_act, (0, 1, 3, 2)).reshape(2 * HN, 32, 64)
    nch = max(1, DN // 4)
    spd = -(-36 // DN)
    np_ = max(1, C // 256)
    sends = DN
    dma = pltpu.SemaphoreType.DMA
    vmem = pl.BlockSpec(memory_space=pltpu.VMEM)
    grad_in, kernel_grad = pl.pallas_call(
        functools.partial(body, DN, C),
        out_shape=(
            jax.ShapeDtypeStruct((128, C), BF),
            jax.ShapeDtypeStruct((27, 32, 32), F32),
        ),
        in_specs=[vmem] * 5,
        out_specs=(vmem, vmem),
        scratch_shapes=[
            pltpu.VMEM((256, C), BF),
            pltpu.VMEM((DN, 32, C), BF),
            pltpu.VMEM((DN, 64, C // 2), BF),
            pltpu.VMEM((64, C // 2), BF),
            pltpu.VMEM((DN, 2, 32, 128), BF),
            pltpu.VMEM((3, HN + 2, 32, 128), BF),
            pltpu.VMEM((3, HN, 96, 128), BF),
            pltpu.VMEM((3, HN + 1, 96, 128), BF),
            pltpu.VMEM((HN, 32, 128), BF),
            pltpu.VMEM((3, 32, 288), F32),
            pltpu.VMEM((3, 32, 288), BF),
            pltpu.VMEM((HN // 4, 32, 512), F32),
            pltpu.VMEM((HN, 32, 128), BF),
            pltpu.VMEM((2, C // 2, 128), BF),
            pltpu.VMEM((3, 32, 384), F32),
            pltpu.VMEM((DN, spd, 8, 128), BF),
            pltpu.VMEM((DN, spd, 8, 128), BF),
            pltpu.VMEM((DN, spd, 8, 128), BF),
            pltpu.VMEM((np_, 128, C // np_), F32),
            pltpu.VMEM((np_, 128, C // np_), F32),
            dma((2,)),
            dma((sends,)),
            dma((DN,)),
            dma((sends,)),
            dma((DN,)),
            dma((DN,)),
            dma((DN,)),
            dma((2, nch)),
            dma((2, nch)),
            dma((DN,)),
            dma((DN,)),
            dma((DN,)),
            dma((DN,)),
            dma((DN,)),
            dma((DN,)),
            dma((np_,)),
            dma((np_,)),
        ],
        compiler_params=pltpu.CompilerParams(
            collective_id=0, has_side_effects=True, vmem_limit_bytes=48 << 20
        ),
    )(rows, turned, w_in, w_out, kernel)
    return grad_in.reshape(grad_out.shape), kernel_grad


def solution(mesh):
    in_specs = (
        P("depth", "height", None, None),
        P("depth", None, None, "height"),
        P("depth", None),
        P("depth", None),
        P(None, None, "height"),
    )
    out_specs = (P("depth", "height", None, None), P(None, None, "height"))
    step = functools.partial(shards, mesh.shape["depth"])
    return jax.shard_map(step, mesh=mesh, in_specs=in_specs, out_specs=out_specs, check_vma=False)
```

```python
import functools

import jax
import jax.numpy as jnp
from jax import lax
from jax.experimental import pallas as pl
from jax.experimental.pallas import tpu as pltpu
from jax.sharding import PartitionSpec as P

MESH = pl.DeviceIdType.MESH
BF = jnp.bfloat16
F32 = jnp.float32


def body(
    DN, C,
    go_hbm, pre_hbm, wi_hbm, wo_hbm, kern_hbm,
    out_hbm, kg_hbm,
    out_ref, kg_ref,
    pre_ref, wi_ref, wo_own, kern_ref, go_buf, wo_buf, wi_buf, wi_own, mt_buf, m_buf, xa, xb, pre2, kmf, kmat, acc, gp_stage, gpr,
    gbuf, g_stage, g_recv, g_fin, p_send, p_recv,
    in_sem, out_sem, go_sem, wo_s, wo_r, wi_s, wi_r, wi_rest, a1_s, a1_r, h_s, h_r, a2_s, a2_r, rs_s, rs_r, ag_s, ag_r, p_s, p_r,
):
    HN = 2 * DN
    Z = DN // 2
    NQ = HN // 4
    NCH = h_r.shape[1]
    KPC = DN // NCH
    SPD = g_stage.shape[1]
    NP = p_send.shape[0]
    PW = C // NP

    d = lax.axis_index("depth")
    h = lax.axis_index("height")
    k = h // 2
    c = h % 2
    xh = d // Z
    z = d % Z

    def remote(src, dst, ss, rs, dd, hh):
        return pltpu.make_async_remote_copy(
            src_ref=src, dst_ref=dst, send_sem=ss, recv_sem=rs, device_id=(dd, hh), device_id_type=MESH
        )

    partner = 2 * k + (1 - c)
    own_cells = pl.ds(pl.multiple_of(128 * c, 128), 128)
    loads = [
        pltpu.make_async_copy(go_hbm, go_buf.at[own_cells, :], in_sem.at[0]),
        pltpu.make_async_copy(wo_hbm.at[pl.ds(pl.multiple_of(32 * c, 32), 32), :], wo_own, in_sem.at[1]),
        pltpu.make_async_copy(kern_hbm, kern_ref, in_sem.at[2]),
        pltpu.make_async_copy(pre_hbm, pre_ref, in_sem.at[3]),
        pltpu.make_async_copy(wi_hbm, wi_ref, in_sem.at[4]),
    ]
    for load in loads:
        load.start()

    barrier = pltpu.get_barrier_semaphore()
    pl.semaphore_signal(barrier, inc=1, device_id=(d, partner), device_id_type=MESH)

    @pl.loop(1, DN)
    def _(j):
        pl.semaphore_signal(barrier, inc=1, device_id=((d + j) % DN, h), device_id_type=MESH)
        pl.semaphore_signal(barrier, inc=1, device_id=(d, 2 * ((k + j) % DN) + c), device_id_type=MESH)

    zero_tile = jnp.zeros((32, 128), BF)
    for s in range(3):
        m_buf[s, 0] = zero_tile
        m_buf[s, HN + 1] = zero_tile

    @pl.when(d == 0)
    def _():
        m_buf[2] = jnp.zeros(m_buf.shape[1:], BF)

    @pl.when(d == DN - 1)
    def _():
        m_buf[0] = jnp.zeros(m_buf.shape[1:], BF)

    for load in loads:
        load.wait()
    for o in range(27):
        s, m = divmod(o, 9)
        kmf[s, :, 32 * m : 32 * m + 32] = kern_ref[o].astype(F32)
    for s in range(3):
        kmat[s] = kmf[s].astype(BF)

    @pl.loop(0, HN)
    def _(t):
        both = jnp.concatenate([pre_ref[2 * t].astype(F32), pre_ref[2 * t + 1].astype(F32)], axis=1)
        pre2[t] = both.astype(BF)

    pl.semaphore_wait(barrier, 1 + 2 * (DN - 1))

    go_copy = remote(go_buf.at[own_cells, :], go_buf.at[own_cells, :], go_sem.at[0], go_sem.at[1], d, partner)
    go_copy.start()

    y = k % Z
    side = k - y
    near_y = (side + (y + 1) % Z, side + (y + Z - 1) % Z)
    held = y % 2

    class Ring:
        def __init__(self, own, buf, view, ss, rs, rest):
            self.own, self.buf, self.view, self.ss, self.rs, self.rest = own, buf, view, ss, rs, rest
            self.first = [(True, 0)]
            self.second = []
            for dz in (2, -2, 1, -1, 3, -3, 4, -4):
                for far in (False, True):
                    limit = Z // 2 if far == (dz < 0) else (Z - 1) // 2
                    if abs(dz) <= limit:
                        (self.first if abs(dz) <= 2 else self.second).append((far, dz))

        def copy(self, src, dst, sem, dd, hh):
            remote(src, dst, self.ss.at[0], sem, dd, hh).start()

        def idx(self, far, dz):
            return (1 - xh if far else xh) * Z + (z + dz + Z) % Z

        def held(self, i):
            return self.view(self.buf.at[i], 2 * held, 2)

        def begin(self):
            mine = self.view(self.own, 2 * held, 2)
            for far, dz in self.first[1:] + self.first[:1]:
                self.copy(mine, self.held(d), self.rs.at[0, d], self.idx(far, dz), h)

        def take(self, far, dz):
            i = self.idx(far, -dz)
            remote(self.held(i), self.held(i), self.ss.at[0], self.rs.at[0, i], d, partner).wait_recv()
            if abs(dz) == 2:
                for other, more in self.second:
                    if other == far and more * dz > 0:
                        self.copy(self.held(i), self.held(i), self.rs.at[0, i], self.idx(False, more - dz), h)

        def share(self, far, dz):
            i = self.idx(far, -dz)
            for e in range(2):
                part = self.view(self.buf.at[i], 2 * held + e, 1)
                self.copy(part, part, self.rest(i), d, 2 * near_y[e] + c)

        def complete(self, far, dz):
            i = self.idx(far, -dz)
            part = self.view(self.buf.at[i], 2 - 2 * held, 2)
            remote(part, part, self.ss.at[0], self.rest(i), d, partner).wait_recv()
            return i

        def finish(self):
            sent = self.buf.at[pl.ds(0, DN - 1)]
            remote(sent, sent, self.ss.at[0], self.rs.at[0, 0], d, partner).wait_send()

    def by_column(ref, first, n):
        return ref.at[:, pl.ds(pl.multiple_of(first * (C // 4), C // 4), n * (C // 4))]

    def by_row(ref, first, n):
        return ref.at[pl.ds(pl.multiple_of(first * 16, 16), n * 16), :]

    ring_o = Ring(wo_own, wo_buf, by_column, wo_s, wo_r, lambda i: wo_r.at[1, i])
    ring_i = Ring(wi_own, wi_buf, by_row, wi_s, wi_r, lambda i: wi_rest.at[0])
    ring_o.begin()

    col = lax.broadcasted_iota(jnp.int32, (C, C // 2), 1)
    row = lax.broadcasted_iota(jnp.int32, (C, C // 2), 0)
    pick = jnp.where(row == 64 * (col // 32) + 32 * c + col % 32, 1.0, 0.0).astype(BF)
    wi_own[...] = jnp.dot(wi_ref[...], pick, preferred_element_type=F32).astype(BF)

    def project(block, i):
        mid = lax.dot_general(block, go_buf[...], (((1,), (1,)), ((), ())), preferred_element_type=F32)
        mid = mid.astype(BF)

        @pl.when(i == k)
        def _():
            m_buf[1, 1 + 2 * i] = mid[:, :128]
            m_buf[1, 2 + 2 * i] = mid[:, 128:]

        @pl.when(i != k)
        def _():
            mt_buf[i, 0] = mid[:, :128]
            mt_buf[i, 1] = mid[:, 128:]
            remote(
                mt_buf.at[i], m_buf.at[1, pl.ds(1 + 2 * k, 2)], a1_s.at[0], a1_r.at[k // KPC], d, 2 * i + c
            ).start()

    go_copy.wait_recv()
    project(wo_own[...], d)
    waiting = []

    def next_block():
        if waiting:
            i = ring_o.complete(*waiting.pop(0))
            project(wo_buf[i], i)

    for far, dz in ring_o.first:
        ring_o.take(far, dz)
        ring_o.share(far, dz)
        waiting.append((far, dz))
        if len(waiting) > 5:
            next_block()
    ring_i.begin()
    for far, dz in ring_o.second:
        ring_o.take(far, dz)
        ring_o.share(far, dz)
        waiting.append((far, dz))
        next_block()
    while waiting:
        next_block()

    up, down = jnp.minimum(d + 1, DN - 1), jnp.maximum(d - 1, 0)

    def halo(n, side):
        part = pl.ds(1 + 2 * KPC * n, 2 * KPC)
        return remote(
            m_buf.at[1, part],
            m_buf.at[2 if side == 0 else 0, part],
            h_s.at[side],
            h_r.at[side, n],
            up if side == 0 else down,
            h,
        )

    for n in range(NCH):
        for there, tiles in ((n != k // KPC, 2 * KPC), (n == k // KPC, 2 * KPC - 2)):
            @pl.when(there)
            def _(n=n, tiles=tiles):
                part = m_buf.at[1, pl.ds(1, tiles)]
                remote(part, part, a1_s.at[0], a1_r.at[n], d, partner).wait_recv()

        @pl.when(d < DN - 1)
        def _(n=n):
            halo(n, 0).start()

        @pl.when(d > 0)
        def _(n=n):
            halo(n, 1).start()

    for far, dz in ring_i.first:
        ring_i.take(far, dz)

    lane = lax.broadcasted_iota(jnp.int32, (4, 32, 128), 2)
    low = lane < 64
    first = lane % 64 == 0
    last = lane % 64 == 63

    def widen(dst, s, at, n, v):
        v0 = v[:n]
        zero = jnp.zeros_like(v0)
        dst[s, pl.ds(at, n), 0:32, :] = jnp.where(last[:n], zero, pltpu.roll(v0, 127, 2)).astype(BF)
        dst[s, pl.ds(at, n), 32:64, :] = v0.astype(BF)
        dst[s, pl.ds(at, n), 64:96, :] = jnp.where(first[:n], zero, pltpu.roll(v0, 1, 2)).astype(BF)

    def spread(s, q):
        here = m_buf[s, pl.ds(1 + 4 * q, 4)].astype(F32)
        before = m_buf[s, pl.ds(4 * q, 4)].astype(F32)
        widen(xa, s, 4 * q, 4, here)
        widen(xb, s, 4 * q, 4, jnp.where(low, pltpu.roll(before, 64, 2), pltpu.roll(here, 64, 2)))

    def spread_next(s, t):
        before = m_buf[s, pl.ds(t, 1)].astype(F32)
        here = m_buf[s, pl.ds(t + 1, 1)].astype(F32)
        widen(xb, s, t, 1, jnp.where(low[:1], pltpu.roll(before, 64, 2), pltpu.roll(here, 64, 2)))

    def columns(s, q):
        tiles = []
        for j in range(4):
            t = 4 * q + j
            tiles.append(jnp.concatenate([xb[s, t + 1], xa[s, t], xb[s, t]], axis=0))
        return jnp.concatenate(tiles, axis=1)

    def hidden(q):
        tiles = [jnp.maximum(pre2[4 * q + j], jnp.zeros((32, 128), BF)) for j in range(4)]
        return jnp.concatenate(tiles, axis=1)

    def outer(x, q):
        return lax.dot_general(hidden(q), x, (((1,), (1,)), ((), ())), preferred_element_type=F32)

    gbuf[...] = jnp.zeros_like(gbuf)

    spread_next(1, HN)

    @pl.loop(0, NQ)
    def _(p):
        q = NQ - 1 - p
        spread(1, q)
        x = columns(1, q)
        acc[q] = jnp.dot(kmat[1], x, preferred_element_type=F32)
        gbuf[1, :, 0:288] += outer(x, q)

    for far, dz in ring_i.first:
        ring_i.share(far, dz)

    for n in range(NCH):
        @pl.when(d < DN - 1)
        def _(n=n):
            halo(n, 1).wait_recv()

        @pl.when(d > 0)
        def _(n=n):
            halo(n, 0).wait_recv()


    @pl.loop(0, NQ)
    def _(p):
        q = (p + k // 2) % NQ
        for s in (0, 2):
            spread(s, q)
            spread_next(s, 4 * q + 4)
        back = acc[q] + jnp.dot(kmat[0], columns(0, q), preferred_element_type=F32)
        back = back + jnp.dot(kmat[2], columns(2, q), preferred_element_type=F32)
        for j in range(4):
            gate = pre2[4 * q + j].astype(F32) > 0
            tile = jnp.where(gate, back[:, 128 * j : 128 * j + 128], jnp.zeros((32, 128), F32))
            gp_stage[4 * q + j] = tile.astype(BF)
        for j in range(2):
            i = 2 * q + j

            @pl.when(i == k)
            def _(i=i):
                for t in range(2):
                    gpr[t, pl.ds(pl.multiple_of(32 * k, 32), 32), :] = gp_stage[2 * i + t]

            @pl.when(i != k)
            def _(i=i):
                remote(
                    gp_stage.at[pl.ds(2 * i, 2)],
                    gpr.at[:, pl.ds(pl.multiple_of(32 * k, 32), 32), :],
                    a2_s.at[0],
                    a2_r.at[0],
                    d,
                    2 * i + c,
                ).start()

    for far, dz in ring_i.second:
        ring_i.take(far, dz)
        ring_i.share(far, dz)

    @pl.loop(0, NQ)
    def _(q):
        gbuf[0, :, 0:288] += outer(columns(0, q), q)
        gbuf[2, :, 0:288] += outer(columns(2, q), q)

    def slot(f):
        return f // SPD, f % SPD

    def cut(f):
        s, rest = divmod(f, 12)
        rb, lt = divmod(rest, 3)
        return s, slice(8 * rb, 8 * rb + 8), slice(128 * lt, 128 * lt + 128)

    for f in range(SPD * DN):
        a, b = slot(f)
        g_stage[a, b] = gbuf[cut(f)].astype(BF) if f < 36 else jnp.zeros((8, 128), BF)

    @pl.loop(1, DN)
    def _(j):
        r = (d + j) % DN
        remote(g_stage.at[r], g_recv.at[d], rs_s.at[0], rs_r.at[0], r, h).start()

    part = g_recv.at[pl.ds(0, DN - 1)]
    remote(part, part, rs_s.at[0], rs_r.at[0], d, partner).wait_recv()
    total = g_stage[d].astype(F32)
    for j in range(1, DN):
        r = (d + j) % DN
        total = total + g_recv[r].astype(F32)
    g_fin[d] = total.astype(BF)

    @pl.loop(1, DN)
    def _(j):
        r = (d + j) % DN
        remote(g_fin.at[d], g_fin.at[d], ag_s.at[0], ag_r.at[0], r, h).start()

    part = wi_buf.at[pl.ds(0, DN - 1), pl.ds(0, 32), :]
    remote(part, part, wi_s.at[0], wi_rest.at[0], d, partner).wait_recv()
    wi_buf[d] = wi_own[...]

    part = gpr.at[:, pl.ds(0, 32 * (DN - 1)), :]
    remote(part, part, a2_s.at[0], a2_r.at[0], d, partner).wait_recv()

    rows_p = wi_buf.shape[0] // NP

    def half(cells, n):
        w = wi_buf[rows_p * n : rows_p * (n + 1)].reshape(PW, C // 2)
        return lax.dot_general(cells, w, (((1,), (1,)), ((), ())), preferred_element_type=F32)

    theirs = gpr[1 - c].T
    exchange = []
    for n in range(NP):
        p_send[n] = half(theirs, n)
        copy = remote(p_send.at[n], p_recv.at[n], p_s.at[0], p_r.at[n], d, partner)
        copy.start()
        exchange.append(copy)

    mine = gpr[c].T
    for n in range(NP):
        part = half(mine, n)
        exchange[n].wait_recv()
        cols = slice(PW * n, PW * (n + 1))
        out_ref[:, cols] = (go_buf[own_cells, cols].astype(F32) + (part + p_recv[n])).astype(BF)
        pltpu.make_async_copy(out_ref.at[:, cols], out_hbm.at[:, cols], out_sem.at[0]).start()

    part = g_fin.at[pl.ds(0, DN - 1)]
    remote(part, part, ag_s.at[0], ag_r.at[0], d, partner).wait_recv()

    scale = float(DN * 2 * HN * 64) ** -0.5
    for f in range(36):
        gbuf[cut(f)] = g_fin[slot(f)].astype(F32) * scale
    for o in range(27):
        s, m = divmod(o, 9)
        kg_ref[o] = gbuf[s, :, 32 * m : 32 * m + 32]

    pltpu.make_async_copy(kg_ref, kg_hbm, out_sem.at[1]).start()

    go_copy.wait_send()
    ring_o.finish()
    ring_i.finish()

    def left(part, sem):
        remote(part, part, sem, go_sem.at[1], d, partner).wait_send()

    left(p_send, p_s.at[0])
    for side, there in ((0, d < DN - 1), (1, d > 0)):
        @pl.when(there)
        def _(side=side):
            left(m_buf.at[1, pl.ds(1, HN)], h_s.at[side])

    left(mt_buf.at[pl.ds(0, DN - 1)], a1_s.at[0])
    left(gp_stage.at[pl.ds(0, 2 * (DN - 1))], a2_s.at[0])
    left(g_stage.at[pl.ds(0, DN - 1)], rs_s.at[0])
    left(g_fin.at[pl.ds(0, DN - 1)], ag_s.at[0])
    pltpu.make_async_copy(out_ref, out_hbm, out_sem.at[0]).wait()
    pltpu.make_async_copy(kg_ref, kg_hbm, out_sem.at[1]).wait()


def shards(DN, grad_out, pre_act, w_in, w_out, kernel):
    C = grad_out.shape[-1]
    HN = 2 * DN
    rows = grad_out.reshape(128, C)
    turned = jnp.transpose(pre_act, (0, 1, 3, 2)).reshape(2 * HN, 32, 64)
    nch = max(1, DN // 4)
    spd = -(-36 // DN)
    np_ = max(1, C // 256)
    dma = pltpu.SemaphoreType.DMA
    grad_in, kernel_grad = pl.pallas_call(
        functools.partial(body, DN, C),
        out_shape=(
            jax.ShapeDtypeStruct((128, C), BF),
            jax.ShapeDtypeStruct((27, 32, 32), F32),
        ),
        in_specs=[pl.BlockSpec(memory_space=pltpu.HBM)] * 5,
        out_specs=(pl.BlockSpec(memory_space=pl.ANY),) * 2,
        scratch_shapes=[
            pltpu.VMEM((128, C), BF),
            pltpu.VMEM((27, 32, 32), F32),
            pltpu.VMEM((2 * HN, 32, 64), BF),
            pltpu.VMEM((64, C), BF),
            pltpu.VMEM((32, C), BF),
            pltpu.VMEM((27, 32, 32), BF),
            pltpu.VMEM((256, C), BF),
            pltpu.VMEM((DN, 32, C), BF),
            pltpu.VMEM((DN, 64, C // 2), BF),
            pltpu.VMEM((64, C // 2), BF),
            pltpu.VMEM((DN, 2, 32, 128), BF),
            pltpu.VMEM((3, HN + 2, 32, 128), BF),
            pltpu.VMEM((3, HN, 96, 128), BF),
            pltpu.VMEM((3, HN + 1, 96, 128), BF),
            pltpu.VMEM((HN, 32, 128), BF),
            pltpu.VMEM((3, 32, 288), F32),
            pltpu.VMEM((3, 32, 288), BF),
            pltpu.VMEM((HN // 4, 32, 512), F32),
            pltpu.VMEM((HN, 32, 128), BF),
            pltpu.VMEM((2, C // 2, 128), BF),
            pltpu.VMEM((3, 32, 384), F32),
            pltpu.VMEM((DN, spd, 8, 128), BF),
            pltpu.VMEM((DN, spd, 8, 128), BF),
            pltpu.VMEM((DN, spd, 8, 128), BF),
            pltpu.VMEM((np_, 128, C // np_), F32),
            pltpu.VMEM((np_, 128, C // np_), F32),
            dma((5,)),
            dma((2,)),
            dma((2,)),
            dma((1,)),
            dma((2, DN)),
            dma((1,)),
            dma((1, DN)),
            dma((1,)),
            dma((1,)),
            dma((nch,)),
            dma((2,)),
            dma((2, nch)),
            dma((1,)),
            dma((1,)),
            dma((1,)),
            dma((1,)),
            dma((1,)),
            dma((1,)),
            dma((1,)),
            dma((np_,)),
        ],
        compiler_params=pltpu.CompilerParams(
            collective_id=0, has_side_effects=True, vmem_limit_bytes=63 << 20
        ),
    )(rows, turned, w_in, w_out, kernel)
    return grad_in.reshape(grad_out.shape), kernel_grad


def solution(mesh):
    in_specs = (
        P("depth", "height", None, None),
        P("depth", None, None, "height"),
        P("depth", None),
        P("depth", None),
        P(None, None, "height"),
    )
    out_specs = (P("depth", "height", None, None), P(None, None, "height"))
    step = functools.partial(shards, mesh.shape["depth"])
    return jax.shard_map(step, mesh=mesh, in_specs=in_specs, out_specs=out_specs, check_vma=False)
```

```python
import functools

import jax
import jax.numpy as jnp
from jax import lax
from jax.experimental import pallas as pl
from jax.experimental.pallas import tpu as pltpu
from jax.sharding import PartitionSpec as P

MESH = pl.DeviceIdType.MESH
BF = jnp.bfloat16
F32 = jnp.float32


def body(
    DN, C,
    go_hbm, pre_hbm, wi_hbm, wo_hbm, kern_hbm,
    out_hbm, kg_hbm,
    out_ref, kg_ref,
    pre_ref, wi_ref, wo_own, kern_ref, go_buf, wo_buf, wi_buf, wi_own, mt_buf, m_buf, xa, xb, pre2, kmf, kmat, acc, gp_stage, gpr,
    gbuf, g_stage, g_recv, g_fin, p_send, p_recv,
    in_sem, out_sem, go_sem, gx_s, gx_r, gf_s, gf_r, wo_s, wo_r, wi_s, wi_r, wi_rest, a1_s, a1_r, h_s, h_r, a2_s, a2_r, rs_s, rs_r, ag_s, ag_r, p_s, p_r,
):
    HN = 2 * DN
    Z = DN // 2
    NQ = HN // 4
    NCH = h_r.shape[1]
    KPC = DN // NCH
    SPD = g_stage.shape[1]
    NP = p_send.shape[0]
    PW = C // NP

    d = lax.axis_index("depth")
    h = lax.axis_index("height")
    k = h // 2
    c = h % 2
    xh = d // Z
    z = d % Z

    def remote(src, dst, ss, rs, dd, hh):
        return pltpu.make_async_remote_copy(
            src_ref=src, dst_ref=dst, send_sem=ss, recv_sem=rs, device_id=(dd, hh), device_id_type=MESH
        )

    xl = k // Z
    y = k % Z
    partner = 2 * k + (1 - c)
    pair = (k + Z) % DN
    own_cells = pl.ds(pl.multiple_of(128 * c, 128), 128)
    loads = [
        pltpu.make_async_copy(go_hbm, go_buf.at[own_cells, :], in_sem.at[0]),
        pltpu.make_async_copy(wo_hbm.at[pl.ds(pl.multiple_of(32 * c, 32), 32), :], wo_own, in_sem.at[1]),
        pltpu.make_async_copy(kern_hbm, kern_ref, in_sem.at[2]),
        pltpu.make_async_copy(pre_hbm, pre_ref, in_sem.at[3]),
        pltpu.make_async_copy(wi_hbm, wi_ref, in_sem.at[4]),
    ]
    for load in loads:
        load.start()

    barrier = pltpu.get_barrier_semaphore()
    pl.semaphore_signal(barrier, inc=1, device_id=(d, partner), device_id_type=MESH)

    @pl.loop(1, DN)
    def _(j):
        pl.semaphore_signal(barrier, inc=1, device_id=((d + j) % DN, h), device_id_type=MESH)
        pl.semaphore_signal(barrier, inc=1, device_id=(d, 2 * ((k + j) % DN) + c), device_id_type=MESH)

    steps = [dz for dz in (2, -2, 1, -1) if (abs(dz) <= Z // 2 if dz > 0 else abs(dz) <= (Z - 1) // 2)]
    across = xh != xl

    def served(dz):
        return xl * Z + (z + dz + Z) % Z, 2 * (xh * Z + y) + c

    @pl.when(across)
    def _():
        for dz in steps + [0]:
            pl.semaphore_signal(barrier, inc=1, device_id=served(dz), device_id_type=MESH)

    zero_tile = jnp.zeros((32, 128), BF)
    for s in range(3):
        m_buf[s, 0] = zero_tile
        m_buf[s, HN + 1] = zero_tile

    @pl.when(d == 0)
    def _():
        m_buf[2] = jnp.zeros(m_buf.shape[1:], BF)

    @pl.when(d == DN - 1)
    def _():
        m_buf[0] = jnp.zeros(m_buf.shape[1:], BF)

    for load in loads:
        load.wait()
    for o in range(27):
        s, m = divmod(o, 9)
        kmf[s, :, 32 * m : 32 * m + 32] = kern_ref[o].astype(F32)
    for s in range(3):
        kmat[s] = kmf[s].astype(BF)

    @pl.loop(0, HN)
    def _(t):
        both = jnp.concatenate([pre_ref[2 * t].astype(F32), pre_ref[2 * t + 1].astype(F32)], axis=1)
        pre2[t] = both.astype(BF)

    pl.semaphore_wait(barrier, 1 + 2 * (DN - 1) + jnp.where(across, len(steps) + 1, 0))

    go_copy = remote(go_buf.at[own_cells, :], go_buf.at[own_cells, :], go_sem.at[0], go_sem.at[1], d, partner)
    go_copy.start()

    NF = gx_r.shape[0]

    def cells(first, n):
        return go_buf.at[pl.ds(pl.multiple_of(first + 128 * c + 128 // NF * n, 128 // NF), 128 // NF), :]

    far_go = [remote(cells(0, n), cells(256, n), gx_s.at[0], gx_r.at[n], d, 2 * pair + c) for n in range(NF)]

    def pass_cells(n):
        far_go[n].wait_recv()
        remote(cells(256, n), cells(256, n), gf_s.at[0], gf_r.at[0], d, partner).start()

    side = k - y
    near_y = (side + (y + 1) % Z, side + (y + Z - 1) % Z)
    held = y % 2

    class Ring:
        def __init__(self, own, buf, view, ss, rs, rest):
            self.own, self.buf, self.view, self.ss, self.rs, self.rest = own, buf, view, ss, rs, rest
            self.first = [(True, 0)]
            self.second = []
            for dz in (2, -2, 1, -1, 3, -3, 4, -4):
                for far in (False, True):
                    limit = Z // 2 if far == (dz < 0) else (Z - 1) // 2
                    if abs(dz) <= limit:
                        (self.first if abs(dz) <= 2 else self.second).append((far, dz))

        def copy(self, src, dst, sem, dd, hh):
            remote(src, dst, self.ss.at[0], sem, dd, hh).start()

        def idx(self, far, dz):
            return (1 - xh if far else xh) * Z + (z + dz + Z) % Z

        def held(self, i):
            return self.view(self.buf.at[i], 2 * held, 2)

        def begin(self):
            mine = self.view(self.own, 2 * held, 2)
            for far, dz in self.first[1:] + self.first[:1]:
                self.copy(mine, self.held(d), self.rs.at[0, d], self.idx(far, dz), h)

        def take(self, far, dz):
            i = self.idx(far, -dz)
            remote(self.held(i), self.held(i), self.ss.at[0], self.rs.at[0, i], d, partner).wait_recv()
            if abs(dz) == 2:
                for other, more in self.second:
                    if other == far and more * dz > 0:
                        self.copy(self.held(i), self.held(i), self.rs.at[0, i], self.idx(False, more - dz), h)

        def share(self, far, dz):
            i = self.idx(far, -dz)
            for e in range(2):
                part = self.view(self.buf.at[i], 2 * held + e, 1)
                self.copy(part, part, self.rest(i), d, 2 * near_y[e] + c)

        def complete(self, far, dz):
            i = self.idx(far, -dz)
            part = self.view(self.buf.at[i], 2 - 2 * held, 2)
            remote(part, part, self.ss.at[0], self.rest(i), d, partner).wait_recv()
            return i

        def finish(self):
            sent = self.buf.at[pl.ds(0, DN - 1)]
            remote(sent, sent, self.ss.at[0], self.rs.at[0, 0], d, partner).wait_send()

    def by_row(ref, first, n):
        return ref.at[pl.ds(pl.multiple_of(first * 16, 16), n * 16), :]


    def send_block(src, dst, i, to):
        remote(src, dst, wo_s.at[0], wo_r.at[i], *to).start()

    for dz in steps:
        send_block(wo_own, wo_buf.at[z], z, served(dz))

    @pl.when(across)
    def _():
        send_block(wo_own, wo_buf.at[z], z, served(0))

    @pl.when(xh == xl)
    def _():
        wo_buf[z] = wo_own[...]

    for copy in far_go:
        copy.start()

    def take_block(dz):
        i = (z - dz + Z) % Z
        whole = wo_buf.at[i]
        remote(whole, whole, wo_s.at[0], wo_r.at[i], d, partner).wait_recv()
        if abs(dz) == 2 and Z >= 8:
            on = dz // 2
            half = whole.at[pl.ds(0 if dz > 0 else 16, 16), :]
            send_block(whole, whole, i, (xh * Z + (z + on + Z) % Z, h))
            send_block(half, half, i, (xh * Z + (z + dz + Z) % Z, h))
        return i

    ring_i = Ring(wi_own, wi_buf, by_row, wi_s, wi_r, lambda i: wi_rest.at[0])
    col = lax.broadcasted_iota(jnp.int32, (C, C // 2), 1)
    row = lax.broadcasted_iota(jnp.int32, (C, C // 2), 0)
    pick = jnp.where(row == 64 * (col // 32) + 32 * c + col % 32, 1.0, 0.0).astype(BF)
    wi_own[...] = jnp.dot(wi_ref[...], pick, preferred_element_type=F32).astype(BF)

    def project(rows, blocks, side):
        mids = lax.dot_general(
            rows, go_buf[256 * side : 256 * side + 256], (((1,), (1,)), ((), ())), preferred_element_type=F32
        ).astype(BF)
        whose = pair if side else k
        part = pl.ds(1 + 2 * whose, 2)
        for n, i in enumerate(blocks):
            mid = mids[32 * n : 32 * n + 32]

            @pl.when(i == y)
            def _(i=i, mid=mid):
                m_buf[1, 1 + 2 * whose] = mid[:, :128]
                m_buf[1, 2 + 2 * whose] = mid[:, 128:]

            @pl.when(i != y)
            def _(i=i, mid=mid):
                at = 2 * i + side
                mt_buf[at, 0] = mid[:, :128]
                mt_buf[at, 1] = mid[:, 128:]
                owner = 2 * (xl * Z + i) + c
                remote(mt_buf.at[at], m_buf.at[1, part], a1_s.at[0], a1_r.at[whose // KPC], d, owner).start()

    def stack(blocks):
        return jnp.concatenate([wo_buf[i] for i in blocks], axis=0)

    go_copy.wait_recv()
    near = [take_block(dz) for dz in steps]
    pass_cells(0)
    pass_cells(1)

    @pl.when(across)
    def _():
        take_block(0)

    near.append(z)
    project(stack(near), near, 0)
    for n in range(2, NF):
        pass_cells(n)
    distant = [take_block(dz) for dz in (3, -3, 4)] if Z >= 8 else []
    ring_i.begin()
    if distant:
        project(stack(distant), distant, 0)
    handed = go_buf.at[pl.ds(0, 128), :]
    remote(handed, handed, gf_s.at[0], gf_r.at[0], d, partner).wait_recv()
    project(wo_buf[...].reshape(32 * Z, C), list(range(Z)), 1)

    up, down = jnp.minimum(d + 1, DN - 1), jnp.maximum(d - 1, 0)

    def halo(n, side):
        part = pl.ds(1 + 2 * KPC * n, 2 * KPC)
        return remote(
            m_buf.at[1, part],
            m_buf.at[2 if side == 0 else 0, part],
            h_s.at[side],
            h_r.at[side, n],
            up if side == 0 else down,
            h,
        )

    turn = [(k // KPC + j) % NCH for j in range(NCH)]
    for j, n in enumerate(turn):
        tiles = 2 * KPC - 2 * (j == 0) - 2 * (j == NCH // 2)
        part = m_buf.at[1, pl.ds(1, tiles)]
        remote(part, part, a1_s.at[0], a1_r.at[n], d, partner).wait_recv()

        @pl.when(d < DN - 1)
        def _(n=n):
            halo(n, 0).start()

        @pl.when(d > 0)
        def _(n=n):
            halo(n, 1).start()

    for far, dz in ring_i.first:
        ring_i.take(far, dz)

    lane = lax.broadcasted_iota(jnp.int32, (4, 32, 128), 2)
    low = lane < 64
    first = lane % 64 == 0
    last = lane % 64 == 63

    def widen(dst, s, at, n, v):
        v0 = v[:n]
        zero = jnp.zeros_like(v0)
        dst[s, pl.ds(at, n), 0:32, :] = jnp.where(last[:n], zero, pltpu.roll(v0, 127, 2)).astype(BF)
        dst[s, pl.ds(at, n), 32:64, :] = v0.astype(BF)
        dst[s, pl.ds(at, n), 64:96, :] = jnp.where(first[:n], zero, pltpu.roll(v0, 1, 2)).astype(BF)

    def spread(s, q):
        here = m_buf[s, pl.ds(1 + 4 * q, 4)].astype(F32)
        before = m_buf[s, pl.ds(4 * q, 4)].astype(F32)
        widen(xa, s, 4 * q, 4, here)
        widen(xb, s, 4 * q, 4, jnp.where(low, pltpu.roll(before, 64, 2), pltpu.roll(here, 64, 2)))

    def spread_next(s, t):
        before = m_buf[s, pl.ds(t, 1)].astype(F32)
        here = m_buf[s, pl.ds(t + 1, 1)].astype(F32)
        widen(xb, s, t, 1, jnp.where(low[:1], pltpu.roll(before, 64, 2), pltpu.roll(here, 64, 2)))

    def columns(s, q):
        tiles = []
        for j in range(4):
            t = 4 * q + j
            tiles.append(jnp.concatenate([xb[s, t + 1], xa[s, t], xb[s, t]], axis=0))
        return jnp.concatenate(tiles, axis=1)

    def hidden(q):
        tiles = [jnp.maximum(pre2[4 * q + j], jnp.zeros((32, 128), BF)) for j in range(4)]
        return jnp.concatenate(tiles, axis=1)

    def outer(x, q):
        return lax.dot_general(hidden(q), x, (((1,), (1,)), ((), ())), preferred_element_type=F32)

    gbuf[...] = jnp.zeros_like(gbuf)

    spread_next(1, HN)

    @pl.loop(0, NQ)
    def _(p):
        q = NQ - 1 - p
        spread(1, q)
        x = columns(1, q)
        acc[q] = jnp.dot(kmat[1], x, preferred_element_type=F32)
        gbuf[1, :, 0:288] += outer(x, q)

    for far, dz in ring_i.first:
        ring_i.share(far, dz)

    def finish_quad(q):
        for s in (0, 2):
            spread(s, q)
            spread_next(s, 4 * q + 4)
        back = acc[q]
        for s in (0, 2):
            x = columns(s, q)
            back = back + jnp.dot(kmat[s], x, preferred_element_type=F32)
            gbuf[s, :, 0:288] += outer(x, q)
        for j in range(4):
            gate = pre2[4 * q + j].astype(F32) > 0
            tile = jnp.where(gate, back[:, 128 * j : 128 * j + 128], jnp.zeros((32, 128), F32))
            gp_stage[4 * q + j] = tile.astype(BF)
        for j in range(2):
            i = 2 * q + j

            @pl.when(i == k)
            def _(i=i):
                for t in range(2):
                    gpr[t, pl.ds(pl.multiple_of(32 * k, 32), 32), :] = gp_stage[2 * i + t]

            @pl.when(i != k)
            def _(i=i):
                remote(
                    gp_stage.at[pl.ds(2 * i, 2)],
                    gpr.at[:, pl.ds(pl.multiple_of(32 * k, 32), 32), :],
                    a2_s.at[0],
                    a2_r.at[0],
                    d,
                    2 * i + c,
                ).start()

    done = 0
    for j, n in enumerate(turn):
        @pl.when(d < DN - 1)
        def _(n=n):
            halo(n, 1).wait_recv()

        @pl.when(d > 0)
        def _(n=n):
            halo(n, 0).wait_recv()

        ready = NQ if j == NCH - 1 else j * (NQ // NCH)
        if ready > done:
            @pl.loop(done, ready)
            def _(p):
                finish_quad((turn[0] * (NQ // NCH) + 1 + p) % NQ)
        done = ready

    def slot(f):
        return f // SPD, f % SPD

    def cut(f):
        s, rest = divmod(f, 12)
        rb, lt = divmod(rest, 3)
        return s, slice(8 * rb, 8 * rb + 8), slice(128 * lt, 128 * lt + 128)

    for f in range(SPD * DN):
        a, b = slot(f)
        g_stage[a, b] = gbuf[cut(f)].astype(BF) if f < 36 else jnp.zeros((8, 128), BF)

    @pl.loop(1, DN)
    def _(j):
        r = (d + j) % DN
        remote(g_stage.at[r], g_recv.at[d], rs_s.at[0], rs_r.at[0], r, h).start()

    for far, dz in ring_i.second:
        ring_i.take(far, dz)
        ring_i.share(far, dz)

    part = g_recv.at[pl.ds(0, DN - 1)]
    remote(part, part, rs_s.at[0], rs_r.at[0], d, partner).wait_recv()
    total = g_stage[d].astype(F32)
    for j in range(1, DN):
        r = (d + j) % DN
        total = total + g_recv[r].astype(F32)
    g_fin[d] = total.astype(BF)

    @pl.loop(1, DN)
    def _(j):
        r = (d + j) % DN
        remote(g_fin.at[d], g_fin.at[d], ag_s.at[0], ag_r.at[0], r, h).start()

    part = wi_buf.at[pl.ds(0, DN - 1), pl.ds(0, 32), :]
    remote(part, part, wi_s.at[0], wi_rest.at[0], d, partner).wait_recv()
    wi_buf[d] = wi_own[...]

    part = gpr.at[:, pl.ds(0, 32 * (DN - 1)), :]
    remote(part, part, a2_s.at[0], a2_r.at[0], d, partner).wait_recv()

    rows_p = wi_buf.shape[0] // NP

    def half(cells, n):
        w = wi_buf[rows_p * n : rows_p * (n + 1)].reshape(PW, C // 2)
        return lax.dot_general(cells, w, (((1,), (1,)), ((), ())), preferred_element_type=F32)

    theirs = gpr[1 - c].T
    exchange = []
    for n in range(NP):
        p_send[n] = half(theirs, n)
        copy = remote(p_send.at[n], p_recv.at[n], p_s.at[0], p_r.at[n], d, partner)
        copy.start()
        exchange.append(copy)

    mine = gpr[c].T
    for n in range(NP):
        part = half(mine, n)
        exchange[n].wait_recv()
        cols = slice(PW * n, PW * (n + 1))
        out_ref[:, cols] = (go_buf[own_cells, cols].astype(F32) + (part + p_recv[n])).astype(BF)
        pltpu.make_async_copy(out_ref.at[:, cols], out_hbm.at[:, cols], out_sem.at[0]).start()

    part = g_fin.at[pl.ds(0, DN - 1)]
    remote(part, part, ag_s.at[0], ag_r.at[0], d, partner).wait_recv()

    scale = float(DN * 2 * HN * 64) ** -0.5
    for f in range(36):
        gbuf[cut(f)] = g_fin[slot(f)].astype(F32) * scale
    for o in range(27):
        s, m = divmod(o, 9)
        kg_ref[o] = gbuf[s, :, 32 * m : 32 * m + 32]

    pltpu.make_async_copy(kg_ref, kg_hbm, out_sem.at[1]).start()

    go_copy.wait_send()
    for there, blocks in ((xh == xl, Z - 1), (across, Z)):
        @pl.when(there)
        def _(blocks=blocks):
            sent = wo_buf.at[pl.ds(0, blocks)]
            remote(sent, sent, wo_s.at[0], wo_r.at[0], d, partner).wait_send()

    ring_i.finish()

    def left(part, sem):
        remote(part, part, sem, go_sem.at[1], d, partner).wait_send()

    left(p_send, p_s.at[0])
    for side, there in ((0, d < DN - 1), (1, d > 0)):
        @pl.when(there)
        def _(side=side):
            left(m_buf.at[1, pl.ds(1, HN)], h_s.at[side])

    left(mt_buf.at[pl.ds(0, DN - 2)], a1_s.at[0])
    left(go_buf.at[pl.ds(0, 128), :], gx_s.at[0])
    left(go_buf.at[pl.ds(0, 128), :], gf_s.at[0])
    left(gp_stage.at[pl.ds(0, 2 * (DN - 1))], a2_s.at[0])
    left(g_stage.at[pl.ds(0, DN - 1)], rs_s.at[0])
    left(g_fin.at[pl.ds(0, DN - 1)], ag_s.at[0])
    pltpu.make_async_copy(out_ref, out_hbm, out_sem.at[0]).wait()
    pltpu.make_async_copy(kg_ref, kg_hbm, out_sem.at[1]).wait()


def shards(DN, grad_out, pre_act, w_in, w_out, kernel):
    C = grad_out.shape[-1]
    HN = 2 * DN
    rows = grad_out.reshape(128, C)
    turned = jnp.transpose(pre_act, (0, 1, 3, 2)).reshape(2 * HN, 32, 64)
    nch = max(1, DN // 4)
    spd = -(-36 // DN)
    np_ = max(1, C // 256)
    dma = pltpu.SemaphoreType.DMA
    grad_in, kernel_grad = pl.pallas_call(
        functools.partial(body, DN, C),
        out_shape=(
            jax.ShapeDtypeStruct((128, C), BF),
            jax.ShapeDtypeStruct((27, 32, 32), F32),
        ),
        in_specs=[pl.BlockSpec(memory_space=pltpu.HBM)] * 5,
        out_specs=(pl.BlockSpec(memory_space=pl.ANY),) * 2,
        scratch_shapes=[
            pltpu.VMEM((128, C), BF),
            pltpu.VMEM((27, 32, 32), F32),
            pltpu.VMEM((2 * HN, 32, 64), BF),
            pltpu.VMEM((64, C), BF),
            pltpu.VMEM((32, C), BF),
            pltpu.VMEM((27, 32, 32), BF),
            pltpu.VMEM((512, C), BF),
            pltpu.VMEM((DN // 2, 32, C), BF),
            pltpu.VMEM((DN, 64, C // 2), BF),
            pltpu.VMEM((64, C // 2), BF),
            pltpu.VMEM((DN, 2, 32, 128), BF),
            pltpu.VMEM((3, HN + 2, 32, 128), BF),
            pltpu.VMEM((3, HN, 96, 128), BF),
            pltpu.VMEM((3, HN + 1, 96, 128), BF),
            pltpu.VMEM((HN, 32, 128), BF),
            pltpu.VMEM((3, 32, 288), F32),
            pltpu.VMEM((3, 32, 288), BF),
            pltpu.VMEM((HN // 4, 32, 512), F32),
            pltpu.VMEM((HN, 32, 128), BF),
            pltpu.VMEM((2, C // 2, 128), BF),
            pltpu.VMEM((3, 32, 384), F32),
            pltpu.VMEM((DN, spd, 8, 128), BF),
            pltpu.VMEM((DN, spd, 8, 128), BF),
            pltpu.VMEM((DN, spd, 8, 128), BF),
            pltpu.VMEM((np_, 128, C // np_), F32),
            pltpu.VMEM((np_, 128, C // np_), F32),
            dma((5,)),
            dma((2,)),
            dma((2,)),
            dma((1,)),
            dma((4,)),
            dma((1,)),
            dma((1,)),
            dma((1,)),
            dma((DN // 2,)),
            dma((1,)),
            dma((1, DN)),
            dma((1,)),
            dma((1,)),
            dma((nch,)),
            dma((2,)),
            dma((2, nch)),
            dma((1,)),
            dma((1,)),
            dma((1,)),
            dma((1,)),
            dma((1,)),
            dma((1,)),
            dma((1,)),
            dma((np_,)),
        ],
        compiler_params=pltpu.CompilerParams(
            collective_id=0, has_side_effects=True, vmem_limit_bytes=63 << 20
        ),
    )(rows, turned, w_in, w_out, kernel)
    return grad_in.reshape(grad_out.shape), kernel_grad


def solution(mesh):
    in_specs = (
        P("depth", "height", None, None),
        P("depth", None, None, "height"),
        P("depth", None),
        P("depth", None),
        P(None, None, "height"),
    )
    out_specs = (P("depth", "height", None, None), P(None, None, "height"))
    step = functools.partial(shards, mesh.shape["depth"])
    return jax.shard_map(step, mesh=mesh, in_specs=in_specs, out_specs=out_specs, check_vma=False)
```

```python
import functools

import jax
import jax.numpy as jnp
from jax import lax
from jax.experimental import pallas as pl
from jax.experimental.pallas import tpu as pltpu
from jax.sharding import PartitionSpec as P

MESH = pl.DeviceIdType.MESH
BF = jnp.bfloat16
F32 = jnp.float32


def body(
    DN, C,
    go_hbm, pre_hbm, wi_hbm, wo_hbm, kern_hbm,
    out_hbm, kg_hbm,
    out_ref, kg_ref,
    pre_ref, wi_ref, wo_own, kern_ref, go_buf, wo_buf, wi_buf, wi_own, mt_buf, m_buf, pre2, kmf, kmat, acc, gp_stage, gpr,
    gbuf, g_stage, g_recv, g_fin, p_send, p_recv,
    in_sem, out_sem, go_sem, gx_s, gx_r, gf_s, gf_r, wo_s, wo_r, wi_s, wi_r, wi_rest, a1_s, a1_r, h_s, h_r, a2_s, a2_r, rs_s, rs_r, ag_s, ag_r, p_s, p_r,
):
    HN = 2 * DN
    Z = DN // 2
    NQ = HN // 4
    NCH = h_r.shape[1]
    KPC = DN // NCH
    SPD = g_stage.shape[1]
    NP = p_send.shape[0]
    PW = C // NP

    d = lax.axis_index("depth")
    h = lax.axis_index("height")
    k = h // 2
    c = h % 2
    xh = d // Z
    z = d % Z

    def remote(src, dst, ss, rs, dd, hh):
        return pltpu.make_async_remote_copy(
            src_ref=src, dst_ref=dst, send_sem=ss, recv_sem=rs, device_id=(dd, hh), device_id_type=MESH
        )

    xl = k // Z
    y = k % Z
    partner = 2 * k + (1 - c)
    pair = (k + Z) % DN
    own_cells = pl.ds(pl.multiple_of(128 * c, 128), 128)
    loads = [
        pltpu.make_async_copy(go_hbm, go_buf.at[own_cells, :], in_sem.at[0]),
        pltpu.make_async_copy(wo_hbm.at[pl.ds(pl.multiple_of(32 * c, 32), 32), :], wo_own, in_sem.at[1]),
        pltpu.make_async_copy(kern_hbm, kern_ref, in_sem.at[2]),
        pltpu.make_async_copy(pre_hbm, pre_ref, in_sem.at[3]),
        pltpu.make_async_copy(wi_hbm, wi_ref, in_sem.at[4]),
    ]
    for load in loads:
        load.start()

    barrier = pltpu.get_barrier_semaphore()
    pl.semaphore_signal(barrier, inc=1, device_id=(d, partner), device_id_type=MESH)

    @pl.loop(1, DN)
    def _(j):
        pl.semaphore_signal(barrier, inc=1, device_id=((d + j) % DN, h), device_id_type=MESH)
        pl.semaphore_signal(barrier, inc=1, device_id=(d, 2 * ((k + j) % DN) + c), device_id_type=MESH)

    steps = [dz for dz in (2, -2, 1, -1) if (abs(dz) <= Z // 2 if dz > 0 else abs(dz) <= (Z - 1) // 2)]
    across = xh != xl

    def served(dz):
        return xl * Z + (z + dz + Z) % Z, 2 * (xh * Z + y) + c

    @pl.when(across)
    def _():
        for dz in steps + [0]:
            pl.semaphore_signal(barrier, inc=1, device_id=served(dz), device_id_type=MESH)

    loads[0].wait()
    loads[1].wait()
    pl.semaphore_wait(barrier, 1 + 2 * (DN - 1) + jnp.where(across, len(steps) + 1, 0))

    go_copy = remote(go_buf.at[own_cells, :], go_buf.at[own_cells, :], go_sem.at[0], go_sem.at[1], d, partner)
    go_copy.start()

    NF = gx_r.shape[0]

    def cells(first, n):
        return go_buf.at[pl.ds(pl.multiple_of(first + 128 * c + 128 // NF * n, 128 // NF), 128 // NF), :]

    far_go = [remote(cells(0, n), cells(256, n), gx_s.at[0], gx_r.at[n], d, 2 * pair + c) for n in range(NF)]

    def pass_cells(n):
        far_go[n].wait_recv()
        remote(cells(256, n), cells(256, n), gf_s.at[0], gf_r.at[0], d, partner).start()

    side = k - y
    near_y = (side + (y + 1) % Z, side + (y + Z - 1) % Z)
    held = y % 2

    class Ring:
        def __init__(self, own, buf, view, ss, rs, rest):
            self.own, self.buf, self.view, self.ss, self.rs, self.rest = own, buf, view, ss, rs, rest
            self.first = [(True, 0)]
            self.second = []
            for dz in (2, -2, 1, -1, 3, -3, 4, -4):
                for far in (False, True):
                    limit = Z // 2 if far == (dz < 0) else (Z - 1) // 2
                    if abs(dz) <= limit:
                        (self.first if abs(dz) <= 2 else self.second).append((far, dz))

        def copy(self, src, dst, sem, dd, hh):
            remote(src, dst, self.ss.at[0], sem, dd, hh).start()

        def idx(self, far, dz):
            return (1 - xh if far else xh) * Z + (z + dz + Z) % Z

        def held(self, i):
            return self.view(self.buf.at[i], 2 * held, 2)

        def begin(self):
            mine = self.view(self.own, 2 * held, 2)
            for far, dz in self.first[1:] + self.first[:1]:
                self.copy(mine, self.held(d), self.rs.at[0, d], self.idx(far, dz), h)

        def take(self, far, dz):
            i = self.idx(far, -dz)
            remote(self.held(i), self.held(i), self.ss.at[0], self.rs.at[0, i], d, partner).wait_recv()
            if abs(dz) == 2:
                for other, more in self.second:
                    if other == far and more * dz > 0:
                        self.copy(self.held(i), self.held(i), self.rs.at[0, i], self.idx(False, more - dz), h)

        def share(self, far, dz):
            i = self.idx(far, -dz)
            for e in range(2):
                part = self.view(self.buf.at[i], 2 * held + e, 1)
                self.copy(part, part, self.rest(i), d, 2 * near_y[e] + c)

        def complete(self, far, dz):
            i = self.idx(far, -dz)
            part = self.view(self.buf.at[i], 2 - 2 * held, 2)
            remote(part, part, self.ss.at[0], self.rest(i), d, partner).wait_recv()
            return i

        def finish(self):
            sent = self.buf.at[pl.ds(0, DN - 1)]
            remote(sent, sent, self.ss.at[0], self.rs.at[0, 0], d, partner).wait_send()

    def by_row(ref, first, n):
        return ref.at[pl.ds(pl.multiple_of(first * 16, 16), n * 16), :]


    def send_block(src, dst, i, to):
        remote(src, dst, wo_s.at[0], wo_r.at[i], *to).start()

    for dz in steps:
        send_block(wo_own, wo_buf.at[z], z, served(dz))

    @pl.when(across)
    def _():
        send_block(wo_own, wo_buf.at[z], z, served(0))

    @pl.when(xh == xl)
    def _():
        wo_buf[z] = wo_own[...]

    for copy in far_go:
        copy.start()

    def take_block(dz):
        i = (z - dz + Z) % Z
        whole = wo_buf.at[i]
        remote(whole, whole, wo_s.at[0], wo_r.at[i], d, partner).wait_recv()
        if abs(dz) == 2 and Z >= 8:
            on = dz // 2
            half = whole.at[pl.ds(0 if dz > 0 else 16, 16), :]
            send_block(whole, whole, i, (xh * Z + (z + on + Z) % Z, h))
            send_block(half, half, i, (xh * Z + (z + dz + Z) % Z, h))
        return i

    ring_i = Ring(wi_own, wi_buf, by_row, wi_s, wi_r, lambda i: wi_rest.at[0])
    def project(rows, blocks, side):
        mids = lax.dot_general(
            rows, go_buf[256 * side : 256 * side + 256], (((1,), (1,)), ((), ())), preferred_element_type=F32
        ).astype(BF)
        whose = pair if side else k
        part = pl.ds(1 + 2 * whose, 2)
        for n, i in enumerate(blocks):
            mid = mids[32 * n : 32 * n + 32]

            @pl.when(i == y)
            def _(i=i, mid=mid):
                m_buf[1, 1 + 2 * whose] = mid[:, :128]
                m_buf[1, 2 + 2 * whose] = mid[:, 128:]

            @pl.when(i != y)
            def _(i=i, mid=mid):
                at = 2 * i + side
                mt_buf[at, 0] = mid[:, :128]
                mt_buf[at, 1] = mid[:, 128:]
                owner = 2 * (xl * Z + i) + c
                remote(mt_buf.at[at], m_buf.at[1, part], a1_s.at[0], a1_r.at[whose // KPC], d, owner).start()

    def stack(blocks):
        return jnp.concatenate([wo_buf[i] for i in blocks], axis=0)

    for load in loads[2:]:
        load.wait()
    zero_tile = jnp.zeros((32, 128), BF)
    for s in range(3):
        m_buf[s, 0] = zero_tile
        m_buf[s, HN + 1] = zero_tile

    @pl.when(d == 0)
    def _():
        m_buf[2] = jnp.zeros(m_buf.shape[1:], BF)

    @pl.when(d == DN - 1)
    def _():
        m_buf[0] = jnp.zeros(m_buf.shape[1:], BF)

    for o in range(27):
        s, m = divmod(o, 9)
        kmf[s, :, 32 * m : 32 * m + 32] = kern_ref[o].astype(F32)
    for s in range(3):
        kmat[s] = kmf[s].astype(BF)

    @pl.loop(0, HN)
    def _(t):
        both = jnp.concatenate([pre_ref[2 * t].astype(F32), pre_ref[2 * t + 1].astype(F32)], axis=1)
        pre2[t] = both.astype(BF)

    col = lax.broadcasted_iota(jnp.int32, (C, C // 2), 1)
    row = lax.broadcasted_iota(jnp.int32, (C, C // 2), 0)
    pick = jnp.where(row == 64 * (col // 32) + 32 * c + col % 32, 1.0, 0.0).astype(BF)
    wi_own[...] = jnp.dot(wi_ref[...], pick, preferred_element_type=F32).astype(BF)

    near = [take_block(dz) for dz in steps]
    pass_cells(0)
    pass_cells(1)

    @pl.when(across)
    def _():
        take_block(0)

    near.append(z)
    go_copy.wait_recv()
    project(stack(near), near, 0)
    for n in range(2, NF):
        pass_cells(n)
    handed = go_buf.at[pl.ds(0, 128), :]
    remote(handed, handed, gf_s.at[0], gf_r.at[0], d, partner).wait_recv()
    project(stack(near), near, 1)
    ring_i.begin()
    if Z >= 8:
        distant = [take_block(dz) for dz in (3, -3, 4)]
        rows = stack(distant)
        project(rows, distant, 0)
        project(rows, distant, 1)
    up, down = jnp.minimum(d + 1, DN - 1), jnp.maximum(d - 1, 0)

    def halo(n, side):
        part = pl.ds(1 + 2 * KPC * n, 2 * KPC)
        return remote(
            m_buf.at[1, part],
            m_buf.at[2 if side == 0 else 0, part],
            h_s.at[side],
            h_r.at[side, n],
            up if side == 0 else down,
            h,
        )

    turn = [(k // KPC + j) % NCH for j in range(NCH)]
    for j, n in enumerate(turn):
        tiles = 2 * KPC - 2 * (j == 0) - 2 * (j == NCH // 2)
        part = m_buf.at[1, pl.ds(1, tiles)]
        remote(part, part, a1_s.at[0], a1_r.at[n], d, partner).wait_recv()

        @pl.when(d < DN - 1)
        def _(n=n):
            halo(n, 0).start()

        @pl.when(d > 0)
        def _(n=n):
            halo(n, 1).start()

    lane = lax.broadcasted_iota(jnp.int32, (5, 32, 128), 2)
    low = lane < 64
    first = lane % 64 == 0
    last = lane % 64 == 63

    def shifts(v):
        n = v.shape[0]
        zero = jnp.zeros_like(v)
        later = jnp.where(last[:n], zero, pltpu.roll(v, 127, 2))
        sooner = jnp.where(first[:n], zero, pltpu.roll(v, 1, 2))
        return later, v, sooner

    def columns(s, q):
        tiles = m_buf[s, pl.ds(4 * q, 6)]
        half = pltpu.roll(tiles, 64, 2)
        even = shifts(tiles[1:5])
        odd = shifts(jnp.where(low, half[0:5], half[1:6]))
        parts = []
        for j in range(4):
            column = [v[j + 1] for v in odd] + [v[j] for v in even] + [v[j] for v in odd]
            parts.append(jnp.concatenate(column, axis=0))
        return jnp.concatenate(parts, axis=1)

    def hidden(q):
        tiles = [jnp.maximum(pre2[4 * q + j], jnp.zeros((32, 128), BF)) for j in range(4)]
        return jnp.concatenate(tiles, axis=1)

    def outer(x, q):
        return lax.dot_general(hidden(q), x, (((1,), (1,)), ((), ())), preferred_element_type=F32)

    gbuf[...] = jnp.zeros_like(gbuf)

    @pl.loop(0, NQ, unroll=min(NQ, 8))
    def _(q):
        x = columns(1, q)
        acc[q] = jnp.dot(kmat[1], x, preferred_element_type=F32)
        gbuf[1, :, 0:288] += outer(x, q)

    def finish_quads(quads):
        for q in quads:
            back = acc[q]
            for s in (0, 2):
                x = columns(s, q)
                back = back + jnp.dot(kmat[s], x, preferred_element_type=F32)
                gbuf[s, :, 0:288] += outer(x, q)
            for j in range(4):
                gate = pre2[4 * q + j].astype(F32) > 0
                tile = jnp.where(gate, back[:, 128 * j : 128 * j + 128], jnp.zeros((32, 128), F32))
                gp_stage[4 * q + j] = tile.astype(BF)
        for q in quads:
            for j in range(2):
                i = 2 * q + j

                @pl.when(i == k)
                def _(i=i):
                    for t in range(2):
                        gpr[t, pl.ds(pl.multiple_of(32 * k, 32), 32), :] = gp_stage[2 * i + t]

                @pl.when(i != k)
                def _(i=i):
                    remote(
                        gp_stage.at[pl.ds(2 * i, 2)],
                        gpr.at[:, pl.ds(pl.multiple_of(32 * k, 32), 32), :],
                        a2_s.at[0],
                        a2_r.at[0],
                        d,
                        2 * i + c,
                    ).start()

    done = 0
    for j, n in enumerate(turn):
        @pl.when(d < DN - 1)
        def _(n=n):
            halo(n, 1).wait_recv()

        @pl.when(d > 0)
        def _(n=n):
            halo(n, 0).wait_recv()

        ready = NQ if j == NCH - 1 else j * (NQ // NCH)
        while done < ready:
            finish_quads([(turn[0] * (NQ // NCH) + 1 + p) % NQ for p in range(done, min(done + 2, ready))])
            done = min(done + 2, ready)
        if j == min(1, NCH - 1):
            for far, dz in ring_i.first:
                ring_i.take(far, dz)
                ring_i.share(far, dz)

    def slot(f):
        return f // SPD, f % SPD

    def cut(f):
        s, rest = divmod(f, 12)
        rb, lt = divmod(rest, 3)
        return s, slice(8 * rb, 8 * rb + 8), slice(128 * lt, 128 * lt + 128)

    for f in range(SPD * DN):
        a, b = slot(f)
        g_stage[a, b] = gbuf[cut(f)].astype(BF) if f < 36 else jnp.zeros((8, 128), BF)

    @pl.loop(1, DN)
    def _(j):
        r = (d + j) % DN
        remote(g_stage.at[r], g_recv.at[d], rs_s.at[0], rs_r.at[0], r, h).start()

    for far, dz in ring_i.second:
        ring_i.take(far, dz)
        ring_i.share(far, dz)

    part = g_recv.at[pl.ds(0, DN - 1)]
    remote(part, part, rs_s.at[0], rs_r.at[0], d, partner).wait_recv()
    total = g_stage[d].astype(F32)
    for j in range(1, DN):
        r = (d + j) % DN
        total = total + g_recv[r].astype(F32)
    g_fin[d] = total.astype(BF)

    @pl.loop(1, DN)
    def _(j):
        r = (d + j) % DN
        remote(g_fin.at[d], g_fin.at[d], ag_s.at[0], ag_r.at[0], r, h).start()

    part = wi_buf.at[pl.ds(0, DN - 1), pl.ds(0, 32), :]
    remote(part, part, wi_s.at[0], wi_rest.at[0], d, partner).wait_recv()
    wi_buf[d] = wi_own[...]

    part = gpr.at[:, pl.ds(0, 32 * (DN - 1)), :]
    remote(part, part, a2_s.at[0], a2_r.at[0], d, partner).wait_recv()

    rows_p = wi_buf.shape[0] // NP

    def half(cells, n):
        w = wi_buf[rows_p * n : rows_p * (n + 1)].reshape(PW, C // 2)
        return lax.dot_general(cells, w, (((1,), (1,)), ((), ())), preferred_element_type=F32)

    theirs = gpr[1 - c].T
    exchange = []
    for n in range(NP):
        p_send[n] = half(theirs, n)
        copy = remote(p_send.at[n], p_recv.at[n], p_s.at[0], p_r.at[n], d, partner)
        copy.start()
        exchange.append(copy)

    mine = gpr[c].T
    for n in range(NP):
        part = half(mine, n)
        exchange[n].wait_recv()
        cols = slice(PW * n, PW * (n + 1))
        out_ref[:, cols] = (go_buf[own_cells, cols].astype(F32) + (part + p_recv[n])).astype(BF)
        pltpu.make_async_copy(out_ref.at[:, cols], out_hbm.at[:, cols], out_sem.at[0]).start()

    part = g_fin.at[pl.ds(0, DN - 1)]
    remote(part, part, ag_s.at[0], ag_r.at[0], d, partner).wait_recv()

    scale = float(DN * 2 * HN * 64) ** -0.5
    for f in range(36):
        gbuf[cut(f)] = g_fin[slot(f)].astype(F32) * scale
    for o in range(27):
        s, m = divmod(o, 9)
        kg_ref[o] = gbuf[s, :, 32 * m : 32 * m + 32]

    pltpu.make_async_copy(kg_ref, kg_hbm, out_sem.at[1]).start()

    go_copy.wait_send()
    for there, blocks in ((xh == xl, Z - 1), (across, Z)):
        @pl.when(there)
        def _(blocks=blocks):
            sent = wo_buf.at[pl.ds(0, blocks)]
            remote(sent, sent, wo_s.at[0], wo_r.at[0], d, partner).wait_send()

    ring_i.finish()

    def left(part, sem):
        remote(part, part, sem, go_sem.at[1], d, partner).wait_send()

    left(p_send, p_s.at[0])
    for side, there in ((0, d < DN - 1), (1, d > 0)):
        @pl.when(there)
        def _(side=side):
            left(m_buf.at[1, pl.ds(1, HN)], h_s.at[side])

    left(mt_buf.at[pl.ds(0, DN - 2)], a1_s.at[0])
    left(go_buf.at[pl.ds(0, 128), :], gx_s.at[0])
    left(go_buf.at[pl.ds(0, 128), :], gf_s.at[0])
    left(gp_stage.at[pl.ds(0, 2 * (DN - 1))], a2_s.at[0])
    left(g_stage.at[pl.ds(0, DN - 1)], rs_s.at[0])
    left(g_fin.at[pl.ds(0, DN - 1)], ag_s.at[0])
    pltpu.make_async_copy(out_ref, out_hbm, out_sem.at[0]).wait()
    pltpu.make_async_copy(kg_ref, kg_hbm, out_sem.at[1]).wait()


def shards(DN, grad_out, pre_act, w_in, w_out, kernel):
    C = grad_out.shape[-1]
    HN = 2 * DN
    rows = grad_out.reshape(128, C)
    turned = jnp.transpose(pre_act, (0, 1, 3, 2)).reshape(2 * HN, 32, 64)
    nch = max(1, DN // 4)
    spd = -(-36 // DN)
    np_ = max(1, C // 256)
    dma = pltpu.SemaphoreType.DMA
    grad_in, kernel_grad = pl.pallas_call(
        functools.partial(body, DN, C),
        out_shape=(
            jax.ShapeDtypeStruct((128, C), BF),
            jax.ShapeDtypeStruct((27, 32, 32), F32),
        ),
        in_specs=[pl.BlockSpec(memory_space=pltpu.HBM)] * 5,
        out_specs=(pl.BlockSpec(memory_space=pl.ANY),) * 2,
        scratch_shapes=[
            pltpu.VMEM((128, C), BF),
            pltpu.VMEM((27, 32, 32), F32),
            pltpu.VMEM((2 * HN, 32, 64), BF),
            pltpu.VMEM((64, C), BF),
            pltpu.VMEM((32, C), BF),
            pltpu.VMEM((27, 32, 32), BF),
            pltpu.VMEM((512, C), BF),
            pltpu.VMEM((DN // 2, 32, C), BF),
            pltpu.VMEM((DN, 64, C // 2), BF),
            pltpu.VMEM((64, C // 2), BF),
            pltpu.VMEM((DN, 2, 32, 128), BF),
            pltpu.VMEM((3, HN + 2, 32, 128), BF),
            pltpu.VMEM((HN, 32, 128), BF),
            pltpu.VMEM((3, 32, 288), F32),
            pltpu.VMEM((3, 32, 288), BF),
            pltpu.VMEM((HN // 4, 32, 512), F32),
            pltpu.VMEM((HN, 32, 128), BF),
            pltpu.VMEM((2, C // 2, 128), BF),
            pltpu.VMEM((3, 32, 384), F32),
            pltpu.VMEM((DN, spd, 8, 128), BF),
            pltpu.VMEM((DN, spd, 8, 128), BF),
            pltpu.VMEM((DN, spd, 8, 128), BF),
            pltpu.VMEM((np_, 128, C // np_), F32),
            pltpu.VMEM((np_, 128, C // np_), F32),
            dma((5,)),
            dma((2,)),
            dma((2,)),
            dma((1,)),
            dma((4,)),
            dma((1,)),
            dma((1,)),
            dma((1,)),
            dma((DN // 2,)),
            dma((1,)),
            dma((1, DN)),
            dma((1,)),
            dma((1,)),
            dma((nch,)),
            dma((2,)),
            dma((2, nch)),
            dma((1,)),
            dma((1,)),
            dma((1,)),
            dma((1,)),
            dma((1,)),
            dma((1,)),
            dma((1,)),
            dma((np_,)),
        ],
        compiler_params=pltpu.CompilerParams(
            collective_id=0, has_side_effects=True, vmem_limit_bytes=63 << 20
        ),
    )(rows, turned, w_in, w_out, kernel)
    return grad_in.reshape(grad_out.shape), kernel_grad


def solution(mesh):
    in_specs = (
        P("depth", "height", None, None),
        P("depth", None, None, "height"),
        P("depth", None),
        P("depth", None),
        P(None, None, "height"),
    )
    out_specs = (P("depth", "height", None, None), P(None, None, "height"))
    step = functools.partial(shards, mesh.shape["depth"])
    return jax.shard_map(step, mesh=mesh, in_specs=in_specs, out_specs=out_specs, check_vma=False)
```

```python
import functools

import jax
import jax.numpy as jnp
from jax import lax
from jax.experimental import pallas as pl
from jax.experimental.pallas import tpu as pltpu
from jax.sharding import PartitionSpec as P

MESH = pl.DeviceIdType.MESH
BF = jnp.bfloat16
F32 = jnp.float32


def body(
    DN, C,
    go_hbm, pre_hbm, wi_hbm, wo_hbm, kern_hbm,
    out_ref, kg_ref,
    pre_ref, wi_ref, wo_own, kern_ref, go_buf, wo_buf, wi_buf, wi_own, mt_buf, m_buf, pre2, kmf, kmat, acc, gp_stage, gpr,
    gbuf, g_stage, g_recv, g_fin, p_send, p_recv,
    in_sem, go_sem, gx_s, gx_r, gf_s, gf_r, wo_s, wo_r, wi_s, wi_r, wi_rest, a1_s, a1_r, h_s, h_r, a2_s, a2_r, rs_s, rs_r, ag_s, ag_r, p_s, p_r,
):
    HN = 2 * DN
    Z = DN // 2
    NQ = HN // 4
    NCH = h_r.shape[1]
    KPC = DN // NCH
    SPD = g_stage.shape[1]
    NP = p_send.shape[0]
    PW = C // NP

    d = lax.axis_index("depth")
    h = lax.axis_index("height")
    k = h // 2
    c = h % 2
    xh = d // Z
    z = d % Z

    def remote(src, dst, ss, rs, dd, hh):
        return pltpu.make_async_remote_copy(
            src_ref=src, dst_ref=dst, send_sem=ss, recv_sem=rs, device_id=(dd, hh), device_id_type=MESH
        )

    xl = k // Z
    y = k % Z
    partner = 2 * k + (1 - c)
    pair = (k + Z) % DN
    own_cells = pl.ds(pl.multiple_of(128 * c, 128), 128)
    loads = [
        pltpu.make_async_copy(go_hbm, go_buf.at[own_cells, :], in_sem.at[0]),
        pltpu.make_async_copy(wo_hbm.at[pl.ds(pl.multiple_of(32 * c, 32), 32), :], wo_own, in_sem.at[1]),
        pltpu.make_async_copy(kern_hbm, kern_ref, in_sem.at[2]),
        pltpu.make_async_copy(pre_hbm, pre_ref, in_sem.at[3]),
        pltpu.make_async_copy(wi_hbm, wi_ref, in_sem.at[4]),
    ]
    for load in loads:
        load.start()

    barrier = pltpu.get_barrier_semaphore()
    pl.semaphore_signal(barrier, inc=1, device_id=(d, partner), device_id_type=MESH)

    @pl.loop(1, DN)
    def _(j):
        pl.semaphore_signal(barrier, inc=1, device_id=((d + j) % DN, h), device_id_type=MESH)
        pl.semaphore_signal(barrier, inc=1, device_id=(d, 2 * ((k + j) % DN) + c), device_id_type=MESH)

    steps = [dz for dz in (2, -2, 1, -1) if (abs(dz) <= Z // 2 if dz > 0 else abs(dz) <= (Z - 1) // 2)]
    across = xh != xl

    def served(dz):
        return xl * Z + (z + dz + Z) % Z, 2 * (xh * Z + y) + c

    @pl.when(across)
    def _():
        for dz in steps + [0]:
            pl.semaphore_signal(barrier, inc=1, device_id=served(dz), device_id_type=MESH)

    loads[0].wait()
    loads[1].wait()
    pl.semaphore_wait(barrier, 1 + 2 * (DN - 1) + jnp.where(across, len(steps) + 1, 0))

    go_copy = remote(go_buf.at[own_cells, :], go_buf.at[own_cells, :], go_sem.at[0], go_sem.at[1], d, partner)
    go_copy.start()

    NF = gx_r.shape[0]

    def cells(first, n):
        return go_buf.at[pl.ds(pl.multiple_of(first + 128 * c + 128 // NF * n, 128 // NF), 128 // NF), :]

    far_go = [remote(cells(0, n), cells(256, n), gx_s.at[0], gx_r.at[n], d, 2 * pair + c) for n in range(NF)]

    def pass_cells(n):
        far_go[n].wait_recv()
        remote(cells(256, n), cells(256, n), gf_s.at[0], gf_r.at[0], d, partner).start()

    side = k - y
    near_y = (side + (y + 1) % Z, side + (y + Z - 1) % Z)
    held = y % 2

    class Ring:
        def __init__(self, own, buf, view, ss, rs, rest):
            self.own, self.buf, self.view, self.ss, self.rs, self.rest = own, buf, view, ss, rs, rest
            self.first = [(True, 0)]
            self.second = []
            for dz in (2, -2, 1, -1, 3, -3, 4, -4):
                for far in (False, True):
                    limit = Z // 2 if far == (dz < 0) else (Z - 1) // 2
                    if abs(dz) <= limit:
                        (self.first if abs(dz) <= 2 else self.second).append((far, dz))

        def copy(self, src, dst, sem, dd, hh):
            remote(src, dst, self.ss.at[0], sem, dd, hh).start()

        def idx(self, far, dz):
            return (1 - xh if far else xh) * Z + (z + dz + Z) % Z

        def held(self, i):
            return self.view(self.buf.at[i], 2 * held, 2)

        def begin(self):
            mine = self.view(self.own, 2 * held, 2)
            for far, dz in self.first[1:] + self.first[:1]:
                self.copy(mine, self.held(d), self.rs.at[0, d], self.idx(far, dz), h)

        def take(self, far, dz):
            i = self.idx(far, -dz)
            remote(self.held(i), self.held(i), self.ss.at[0], self.rs.at[0, i], d, partner).wait_recv()
            if abs(dz) == 2:
                for other, more in self.second:
                    if other == far and more * dz > 0:
                        self.copy(self.held(i), self.held(i), self.rs.at[0, i], self.idx(False, more - dz), h)

        def share(self, far, dz):
            i = self.idx(far, -dz)
            for e in range(2):
                part = self.view(self.buf.at[i], 2 * held + e, 1)
                self.copy(part, part, self.rest(i), d, 2 * near_y[e] + c)

        def complete(self, far, dz):
            i = self.idx(far, -dz)
            part = self.view(self.buf.at[i], 2 - 2 * held, 2)
            remote(part, part, self.ss.at[0], self.rest(i), d, partner).wait_recv()
            return i

        def finish(self):
            sent = self.buf.at[pl.ds(0, DN - 1)]
            remote(sent, sent, self.ss.at[0], self.rs.at[0, 0], d, partner).wait_send()

    def by_row(ref, first, n):
        return ref.at[pl.ds(pl.multiple_of(first * 16, 16), n * 16), :]


    def send_block(src, dst, i, to):
        remote(src, dst, wo_s.at[0], wo_r.at[i], *to).start()

    for dz in steps:
        send_block(wo_own, wo_buf.at[z], z, served(dz))

    @pl.when(across)
    def _():
        send_block(wo_own, wo_buf.at[z], z, served(0))

    @pl.when(xh == xl)
    def _():
        wo_buf[z] = wo_own[...]

    for copy in far_go:
        copy.start()

    def take_block(dz):
        i = (z - dz + Z) % Z
        whole = wo_buf.at[i]
        remote(whole, whole, wo_s.at[0], wo_r.at[i], d, partner).wait_recv()
        if abs(dz) == 2 and Z >= 8:
            on = dz // 2
            half = whole.at[pl.ds(0 if dz > 0 else 16, 16), :]
            send_block(whole, whole, i, (xh * Z + (z + on + Z) % Z, h))
            send_block(half, half, i, (xh * Z + (z + dz + Z) % Z, h))
        return i

    ring_i = Ring(wi_own, wi_buf, by_row, wi_s, wi_r, lambda i: wi_rest.at[0])
    def project(rows, blocks, side):
        mids = lax.dot_general(
            rows, go_buf[256 * side : 256 * side + 256], (((1,), (1,)), ((), ())), preferred_element_type=F32
        ).astype(BF)
        whose = pair if side else k
        part = pl.ds(1 + 2 * whose, 2)
        for n, i in enumerate(blocks):
            mid = mids[32 * n : 32 * n + 32]

            @pl.when(i == y)
            def _(i=i, mid=mid):
                m_buf[1, 1 + 2 * whose] = mid[:, :128]
                m_buf[1, 2 + 2 * whose] = mid[:, 128:]

            @pl.when(i != y)
            def _(i=i, mid=mid):
                at = 2 * i + side
                mt_buf[at, 0] = mid[:, :128]
                mt_buf[at, 1] = mid[:, 128:]
                owner = 2 * (xl * Z + i) + c
                remote(mt_buf.at[at], m_buf.at[1, part], a1_s.at[0], a1_r.at[whose // KPC], d, owner).start()

    def stack(blocks):
        return jnp.concatenate([wo_buf[i] for i in blocks], axis=0)

    for load in loads[2:]:
        load.wait()
    zero_tile = jnp.zeros((32, 128), BF)
    for s in range(3):
        m_buf[s, 0] = zero_tile
        m_buf[s, HN + 1] = zero_tile

    @pl.when(d == 0)
    def _():
        m_buf[2] = jnp.zeros(m_buf.shape[1:], BF)

    @pl.when(d == DN - 1)
    def _():
        m_buf[0] = jnp.zeros(m_buf.shape[1:], BF)

    for o in range(27):
        s, m = divmod(o, 9)
        kmf[s, :, 32 * m : 32 * m + 32] = kern_ref[o].astype(F32)
    for s in range(3):
        kmat[s] = kmf[s].astype(BF)

    @pl.loop(0, HN)
    def _(t):
        both = jnp.concatenate([pre_ref[2 * t].astype(F32), pre_ref[2 * t + 1].astype(F32)], axis=1)
        pre2[t] = both.astype(BF)

    col = lax.broadcasted_iota(jnp.int32, (C, C // 2), 1)
    row = lax.broadcasted_iota(jnp.int32, (C, C // 2), 0)
    pick = jnp.where(row == 64 * (col // 32) + 32 * c + col % 32, 1.0, 0.0).astype(BF)
    wi_own[...] = jnp.dot(wi_ref[...], pick, preferred_element_type=F32).astype(BF)

    near = [take_block(dz) for dz in steps]
    pass_cells(0)
    pass_cells(1)

    @pl.when(across)
    def _():
        take_block(0)

    near.append(z)
    go_copy.wait_recv()
    project(stack(near), near, 0)
    for n in range(2, NF):
        pass_cells(n)
    handed = go_buf.at[pl.ds(0, 128), :]
    remote(handed, handed, gf_s.at[0], gf_r.at[0], d, partner).wait_recv()
    project(stack(near), near, 1)
    ring_i.begin()
    if Z >= 8:
        distant = [take_block(dz) for dz in (3, -3, 4)]
        rows = stack(distant)
        project(rows, distant, 0)
        project(rows, distant, 1)
    up, down = jnp.minimum(d + 1, DN - 1), jnp.maximum(d - 1, 0)

    def halo(n, side):
        part = pl.ds(1 + 2 * KPC * n, 2 * KPC)
        return remote(
            m_buf.at[1, part],
            m_buf.at[2 if side == 0 else 0, part],
            h_s.at[side],
            h_r.at[side, n],
            up if side == 0 else down,
            h,
        )

    turn = [(k // KPC + j) % NCH for j in range(NCH)]
    for j, n in enumerate(turn):
        tiles = 2 * KPC - 2 * (j == 0) - 2 * (j == NCH // 2)
        part = m_buf.at[1, pl.ds(1, tiles)]
        remote(part, part, a1_s.at[0], a1_r.at[n], d, partner).wait_recv()

        @pl.when(d < DN - 1)
        def _(n=n):
            halo(n, 0).start()

        @pl.when(d > 0)
        def _(n=n):
            halo(n, 1).start()

    lane = lax.broadcasted_iota(jnp.int32, (5, 32, 128), 2)
    low = lane < 64
    first = lane % 64 == 0
    last = lane % 64 == 63

    def shifts(v):
        n = v.shape[0]
        zero = jnp.zeros_like(v)
        later = jnp.where(last[:n], zero, pltpu.roll(v, 127, 2))
        sooner = jnp.where(first[:n], zero, pltpu.roll(v, 1, 2))
        return later, v, sooner

    def columns(s, q):
        tiles = m_buf[s, pl.ds(4 * q, 6)]
        half = pltpu.roll(tiles, 64, 2)
        even = shifts(tiles[1:5])
        odd = shifts(jnp.where(low, half[0:5], half[1:6]))
        parts = []
        for j in range(4):
            column = [v[j + 1] for v in odd] + [v[j] for v in even] + [v[j] for v in odd]
            parts.append(jnp.concatenate(column, axis=0))
        return jnp.concatenate(parts, axis=1)

    def hidden(q):
        tiles = [jnp.maximum(pre2[4 * q + j], jnp.zeros((32, 128), BF)) for j in range(4)]
        return jnp.concatenate(tiles, axis=1)

    def outer(x, q):
        return lax.dot_general(hidden(q), x, (((1,), (1,)), ((), ())), preferred_element_type=F32)

    gbuf[...] = jnp.zeros_like(gbuf)

    @pl.loop(0, NQ, unroll=min(NQ, 8))
    def _(q):
        x = columns(1, q)
        acc[q] = jnp.dot(kmat[1], x, preferred_element_type=F32)
        gbuf[1, :, 0:288] += outer(x, q)

    def finish_quads(quads):
        for q in quads:
            back = acc[q]
            for s in (0, 2):
                x = columns(s, q)
                back = back + jnp.dot(kmat[s], x, preferred_element_type=F32)
                gbuf[s, :, 0:288] += outer(x, q)
            for j in range(4):
                gate = pre2[4 * q + j].astype(F32) > 0
                tile = jnp.where(gate, back[:, 128 * j : 128 * j + 128], jnp.zeros((32, 128), F32))
                gp_stage[4 * q + j] = tile.astype(BF)
        for q in quads:
            for j in range(2):
                i = 2 * q + j

                @pl.when(i == k)
                def _(i=i):
                    for t in range(2):
                        gpr[t, pl.ds(pl.multiple_of(32 * k, 32), 32), :] = gp_stage[2 * i + t]

                @pl.when(i != k)
                def _(i=i):
                    remote(
                        gp_stage.at[pl.ds(2 * i, 2)],
                        gpr.at[:, pl.ds(pl.multiple_of(32 * k, 32), 32), :],
                        a2_s.at[0],
                        a2_r.at[0],
                        d,
                        2 * i + c,
                    ).start()

    done = 0
    for j, n in enumerate(turn):
        @pl.when(d < DN - 1)
        def _(n=n):
            halo(n, 1).wait_recv()

        @pl.when(d > 0)
        def _(n=n):
            halo(n, 0).wait_recv()

        ready = NQ if j == NCH - 1 else j * (NQ // NCH)
        while done < ready:
            finish_quads([(turn[0] * (NQ // NCH) + 1 + p) % NQ for p in range(done, min(done + 2, ready))])
            done = min(done + 2, ready)
        if j == min(1, NCH - 1):
            for far, dz in ring_i.first:
                ring_i.take(far, dz)
                ring_i.share(far, dz)

    def slot(f):
        return f // SPD, f % SPD

    def cut(f):
        s, rest = divmod(f, 12)
        rb, lt = divmod(rest, 3)
        return s, slice(8 * rb, 8 * rb + 8), slice(128 * lt, 128 * lt + 128)

    for f in range(SPD * DN):
        a, b = slot(f)
        g_stage[a, b] = gbuf[cut(f)].astype(BF) if f < 36 else jnp.zeros((8, 128), BF)

    @pl.loop(1, DN)
    def _(j):
        r = (d + j) % DN
        remote(g_stage.at[r], g_recv.at[d], rs_s.at[0], rs_r.at[0], r, h).start()

    for far, dz in ring_i.second:
        ring_i.take(far, dz)
        ring_i.share(far, dz)

    part = g_recv.at[pl.ds(0, DN - 1)]
    remote(part, part, rs_s.at[0], rs_r.at[0], d, partner).wait_recv()
    total = g_stage[d].astype(F32)
    for j in range(1, DN):
        r = (d + j) % DN
        total = total + g_recv[r].astype(F32)
    g_fin[d] = total.astype(BF)

    @pl.loop(1, DN)
    def _(j):
        r = (d + j) % DN
        remote(g_fin.at[d], g_fin.at[d], ag_s.at[0], ag_r.at[0], r, h).start()

    part = wi_buf.at[pl.ds(0, DN - 1), pl.ds(0, 32), :]
    remote(part, part, wi_s.at[0], wi_rest.at[0], d, partner).wait_recv()
    wi_buf[d] = wi_own[...]

    part = gpr.at[:, pl.ds(0, 32 * (DN - 1)), :]
    remote(part, part, a2_s.at[0], a2_r.at[0], d, partner).wait_recv()

    rows_p = wi_buf.shape[0] // NP

    def half(cells, n):
        w = wi_buf[rows_p * n : rows_p * (n + 1)].reshape(PW, C // 2)
        return lax.dot_general(cells, w, (((1,), (1,)), ((), ())), preferred_element_type=F32)

    theirs = gpr[1 - c].T
    exchange = []
    for n in range(NP):
        p_send[n] = half(theirs, n)
        copy = remote(p_send.at[n], p_recv.at[n], p_s.at[0], p_r.at[n], d, partner)
        copy.start()
        exchange.append(copy)

    mine = gpr[c].T
    for n in range(NP):
        part = half(mine, n)
        exchange[n].wait_recv()
        cols = slice(PW * n, PW * (n + 1))
        out_ref[:, cols] = (go_buf[own_cells, cols].astype(F32) + (part + p_recv[n])).astype(BF)

    part = g_fin.at[pl.ds(0, DN - 1)]
    remote(part, part, ag_s.at[0], ag_r.at[0], d, partner).wait_recv()

    scale = float(DN * 2 * HN * 64) ** -0.5
    for f in range(36):
        gbuf[cut(f)] = g_fin[slot(f)].astype(F32) * scale
    for o in range(27):
        s, m = divmod(o, 9)
        kg_ref[o] = gbuf[s, :, 32 * m : 32 * m + 32]


    go_copy.wait_send()
    for there, blocks in ((xh == xl, Z - 1), (across, Z)):
        @pl.when(there)
        def _(blocks=blocks):
            sent = wo_buf.at[pl.ds(0, blocks)]
            remote(sent, sent, wo_s.at[0], wo_r.at[0], d, partner).wait_send()

    ring_i.finish()

    def left(part, sem):
        remote(part, part, sem, go_sem.at[1], d, partner).wait_send()

    left(p_send, p_s.at[0])
    for side, there in ((0, d < DN - 1), (1, d > 0)):
        @pl.when(there)
        def _(side=side):
            left(m_buf.at[1, pl.ds(1, HN)], h_s.at[side])

    left(mt_buf.at[pl.ds(0, DN - 2)], a1_s.at[0])
    left(go_buf.at[pl.ds(0, 128), :], gx_s.at[0])
    left(go_buf.at[pl.ds(0, 128), :], gf_s.at[0])
    left(gp_stage.at[pl.ds(0, 2 * (DN - 1))], a2_s.at[0])
    left(g_stage.at[pl.ds(0, DN - 1)], rs_s.at[0])
    left(g_fin.at[pl.ds(0, DN - 1)], ag_s.at[0])


def shards(DN, grad_out, pre_act, w_in, w_out, kernel):
    C = grad_out.shape[-1]
    HN = 2 * DN
    rows = grad_out.reshape(128, C)
    turned = jnp.transpose(pre_act, (0, 1, 3, 2)).reshape(2 * HN, 32, 64)
    nch = max(1, DN // 4)
    spd = -(-36 // DN)
    np_ = max(1, C // 256)
    dma = pltpu.SemaphoreType.DMA
    grad_in, kernel_grad = pl.pallas_call(
        functools.partial(body, DN, C),
        out_shape=(
            pltpu.VMEM((128, C), BF),
            pltpu.VMEM((27, 32, 32), F32),
        ),
        in_specs=[pl.BlockSpec(memory_space=pltpu.HBM)] * 5,
        out_specs=(pl.BlockSpec(memory_space=pltpu.VMEM),) * 2,
        scratch_shapes=[
            pltpu.VMEM((2 * HN, 32, 64), BF),
            pltpu.VMEM((64, C), BF),
            pltpu.VMEM((32, C), BF),
            pltpu.VMEM((27, 32, 32), BF),
            pltpu.VMEM((512, C), BF),
            pltpu.VMEM((DN // 2, 32, C), BF),
            pltpu.VMEM((DN, 64, C // 2), BF),
            pltpu.VMEM((64, C // 2), BF),
            pltpu.VMEM((DN, 2, 32, 128), BF),
            pltpu.VMEM((3, HN + 2, 32, 128), BF),
            pltpu.VMEM((HN, 32, 128), BF),
            pltpu.VMEM((3, 32, 288), F32),
            pltpu.VMEM((3, 32, 288), BF),
            pltpu.VMEM((HN // 4, 32, 512), F32),
            pltpu.VMEM((HN, 32, 128), BF),
            pltpu.VMEM((2, C // 2, 128), BF),
            pltpu.VMEM((3, 32, 384), F32),
            pltpu.VMEM((DN, spd, 8, 128), BF),
            pltpu.VMEM((DN, spd, 8, 128), BF),
            pltpu.VMEM((DN, spd, 8, 128), BF),
            pltpu.VMEM((np_, 128, C // np_), F32),
            pltpu.VMEM((np_, 128, C // np_), F32),
            dma((5,)),
            dma((2,)),
            dma((1,)),
            dma((4,)),
            dma((1,)),
            dma((1,)),
            dma((1,)),
            dma((DN // 2,)),
            dma((1,)),
            dma((1, DN)),
            dma((1,)),
            dma((1,)),
            dma((nch,)),
            dma((2,)),
            dma((2, nch)),
            dma((1,)),
            dma((1,)),
            dma((1,)),
            dma((1,)),
            dma((1,)),
            dma((1,)),
            dma((1,)),
            dma((np_,)),
        ],
        compiler_params=pltpu.CompilerParams(
            collective_id=0, has_side_effects=True, vmem_limit_bytes=63 << 20
        ),
    )(rows, turned, w_in, w_out, kernel)
    return grad_in.reshape(grad_out.shape), kernel_grad


def solution(mesh):
    in_specs = (
        P("depth", "height", None, None),
        P("depth", None, None, "height"),
        P("depth", None),
        P("depth", None),
        P(None, None, "height"),
    )
    out_specs = (P("depth", "height", None, None), P(None, None, "height"))
    step = functools.partial(shards, mesh.shape["depth"])
    return jax.shard_map(step, mesh=mesh, in_specs=in_specs, out_specs=out_specs, check_vma=False)
```

```python
import functools

import jax
import jax.numpy as jnp
from jax import lax
from jax.experimental import pallas as pl
from jax.experimental.pallas import tpu as pltpu
from jax.sharding import PartitionSpec as P

MESH = pl.DeviceIdType.MESH
BF = jnp.bfloat16
F32 = jnp.float32


def body(
    DN, C,
    go_hbm, pre_hbm, wi_hbm, wo_hbm, kern_hbm,
    out_ref, kg_ref,
    pre_ref, wi_ref, wo_own, kern_ref, go_buf, wo_buf, wi_buf, wi_own, mt_buf, m_buf, pre2, kmf, kmat, acc, gp_stage, gpr,
    gbuf, g_stage, g_recv, g_fin, p_send, p_recv,
    in_sem, go_sem, gx_s, gx_r, gf_s, gf_r, wo_s, wo_r, wi_s, wi_r, wi_rest, a1_s, a1_r, h_s, h_r, a2_s, a2_r, rs_s, rs_r, ag_s, ag_r, p_s, p_r,
):
    HN = 2 * DN
    Z = DN // 2
    NQ = HN // 4
    NCH = h_r.shape[1]
    KPC = DN // NCH
    SPD = g_stage.shape[1]
    NP = p_send.shape[0]
    PW = C // NP

    d = lax.axis_index("depth")
    h = lax.axis_index("height")
    k = h // 2
    c = h % 2
    xh = d // Z
    z = d % Z

    def remote(src, dst, ss, rs, dd, hh):
        return pltpu.make_async_remote_copy(
            src_ref=src, dst_ref=dst, send_sem=ss, recv_sem=rs, device_id=(dd, hh), device_id_type=MESH
        )

    xl = k // Z
    y = k % Z
    partner = 2 * k + (1 - c)
    pair = (k + Z) % DN
    own_cells = pl.ds(pl.multiple_of(128 * c, 128), 128)
    loads = [
        pltpu.make_async_copy(go_hbm, go_buf.at[own_cells, :], in_sem.at[0]),
        pltpu.make_async_copy(wo_hbm.at[pl.ds(pl.multiple_of(32 * c, 32), 32), :], wo_own, in_sem.at[1]),
        pltpu.make_async_copy(kern_hbm, kern_ref, in_sem.at[2]),
        pltpu.make_async_copy(pre_hbm, pre_ref, in_sem.at[3]),
        pltpu.make_async_copy(wi_hbm, wi_ref, in_sem.at[4]),
    ]
    for load in loads:
        load.start()

    barrier = pltpu.get_barrier_semaphore()
    pl.semaphore_signal(barrier, inc=1, device_id=(d, partner), device_id_type=MESH)

    @pl.loop(1, DN)
    def _(step):
        j = (step + 3 * DN // 4 - 2) % (DN - 1) + 1
        pl.semaphore_signal(barrier, inc=1, device_id=((d + j) % DN, h), device_id_type=MESH)
        pl.semaphore_signal(barrier, inc=1, device_id=(d, 2 * ((k + j) % DN) + c), device_id_type=MESH)

    steps = [dz for dz in (2, -2, 1, -1) if (abs(dz) <= Z // 2 if dz > 0 else abs(dz) <= (Z - 1) // 2)]
    across = xh != xl

    def served(dz):
        return xl * Z + (z + dz + Z) % Z, 2 * (xh * Z + y) + c

    @pl.when(across)
    def _():
        for dz in steps + [0]:
            pl.semaphore_signal(barrier, inc=1, device_id=served(dz), device_id_type=MESH)

    loads[0].wait()
    loads[1].wait()
    pl.semaphore_wait(barrier, 1 + 2 * (DN - 1) + jnp.where(across, len(steps) + 1, 0))

    go_copy = remote(go_buf.at[own_cells, :], go_buf.at[own_cells, :], go_sem.at[0], go_sem.at[1], d, partner)
    go_copy.start()

    NF = gx_r.shape[0]

    def cells(first, n):
        return go_buf.at[pl.ds(pl.multiple_of(first + 128 * c + 128 // NF * n, 128 // NF), 128 // NF), :]

    far_go = [remote(cells(0, n), cells(256, n), gx_s.at[0], gx_r.at[n], d, 2 * pair + c) for n in range(NF)]

    def pass_cells(n):
        far_go[n].wait_recv()
        remote(cells(256, n), cells(256, n), gf_s.at[0], gf_r.at[0], d, partner).start()

    side = k - y
    near_y = (side + (y + 1) % Z, side + (y + Z - 1) % Z)
    held = y % 2

    class Ring:
        def __init__(self, own, buf, view, ss, rs, rest):
            self.own, self.buf, self.view, self.ss, self.rs, self.rest = own, buf, view, ss, rs, rest
            self.first = [(True, 0)]
            self.second = []
            for dz in (2, -2, 1, -1, 3, -3, 4, -4):
                for far in (False, True):
                    limit = Z // 2 if far == (dz < 0) else (Z - 1) // 2
                    if abs(dz) <= limit:
                        (self.first if abs(dz) <= 2 else self.second).append((far, dz))

        def copy(self, src, dst, sem, dd, hh):
            remote(src, dst, self.ss.at[0], sem, dd, hh).start()

        def idx(self, far, dz):
            return (1 - xh if far else xh) * Z + (z + dz + Z) % Z

        def held(self, i):
            return self.view(self.buf.at[i], 2 * held, 2)

        def begin(self):
            mine = self.view(self.own, 2 * held, 2)
            for far, dz in self.first[1:] + self.first[:1]:
                self.copy(mine, self.held(d), self.rs.at[0, d], self.idx(far, dz), h)

        def take(self, far, dz):
            i = self.idx(far, -dz)
            remote(self.held(i), self.held(i), self.ss.at[0], self.rs.at[0, i], d, partner).wait_recv()
            if abs(dz) == 2:
                for other, more in self.second:
                    if other == far and more * dz > 0:
                        self.copy(self.held(i), self.held(i), self.rs.at[0, i], self.idx(False, more - dz), h)

        def share(self, far, dz):
            i = self.idx(far, -dz)
            for e in range(2):
                part = self.view(self.buf.at[i], 2 * held + e, 1)
                self.copy(part, part, self.rest(i), d, 2 * near_y[e] + c)

        def complete(self, far, dz):
            i = self.idx(far, -dz)
            part = self.view(self.buf.at[i], 2 - 2 * held, 2)
            remote(part, part, self.ss.at[0], self.rest(i), d, partner).wait_recv()
            return i

        def finish(self):
            sent = self.buf.at[pl.ds(0, DN - 1)]
            remote(sent, sent, self.ss.at[0], self.rs.at[0, 0], d, partner).wait_send()

    def by_row(ref, first, n):
        return ref.at[pl.ds(pl.multiple_of(first * 16, 16), n * 16), :]


    def send_block(src, dst, i, to):
        remote(src, dst, wo_s.at[0], wo_r.at[i], *to).start()

    for dz in steps[:2]:
        send_block(wo_own, wo_buf.at[z], z, served(dz))

    @pl.when(xh == xl)
    def _():
        wo_buf[z] = wo_own[...]

    for copy in far_go:
        copy.start()

    def take_block(dz):
        i = (z - dz + Z) % Z
        whole = wo_buf.at[i]
        remote(whole, whole, wo_s.at[0], wo_r.at[i], d, partner).wait_recv()
        if abs(dz) == 2 and Z >= 8:
            on = dz // 2
            half = whole.at[pl.ds(0 if dz > 0 else 16, 16), :]
            send_block(whole, whole, i, (xh * Z + (z + on + Z) % Z, h))
            send_block(half, half, i, (xh * Z + (z + dz + Z) % Z, h))
        return i

    ring_i = Ring(wi_own, wi_buf, by_row, wi_s, wi_r, lambda i: wi_rest.at[0])
    def project(rows, blocks, side):
        mids = lax.dot_general(
            rows, go_buf[256 * side : 256 * side + 256], (((1,), (1,)), ((), ())), preferred_element_type=F32
        ).astype(BF)
        whose = pair if side else k
        part = pl.ds(1 + 2 * whose, 2)
        for n, i in enumerate(blocks):
            mid = mids[32 * n : 32 * n + 32]

            @pl.when(i == y)
            def _(i=i, mid=mid):
                m_buf[1, 1 + 2 * whose] = mid[:, :128]
                m_buf[1, 2 + 2 * whose] = mid[:, 128:]

            @pl.when(i != y)
            def _(i=i, mid=mid):
                at = 2 * i + side
                mt_buf[at, 0] = mid[:, :128]
                mt_buf[at, 1] = mid[:, 128:]
                owner = 2 * (xl * Z + i) + c
                remote(mt_buf.at[at], m_buf.at[1, part], a1_s.at[0], a1_r.at[whose // KPC], d, owner).start()

    def stack(blocks):
        return jnp.concatenate([wo_buf[i] for i in blocks], axis=0)

    for load in loads[2:]:
        load.wait()
    zero_tile = jnp.zeros((32, 128), BF)
    for s in range(3):
        m_buf[s, 0] = zero_tile
        m_buf[s, HN + 1] = zero_tile

    @pl.when(d == 0)
    def _():
        m_buf[2] = jnp.zeros(m_buf.shape[1:], BF)

    @pl.when(d == DN - 1)
    def _():
        m_buf[0] = jnp.zeros(m_buf.shape[1:], BF)

    for o in range(27):
        s, m = divmod(o, 9)
        kmf[s, :, 32 * m : 32 * m + 32] = kern_ref[o].astype(F32)
    for s in range(3):
        kmat[s] = kmf[s].astype(BF)

    for dz in steps[2:]:
        send_block(wo_own, wo_buf.at[z], z, served(dz))

    @pl.when(across)
    def _():
        send_block(wo_own, wo_buf.at[z], z, served(0))

    @pl.loop(0, HN)
    def _(t):
        both = jnp.concatenate([pre_ref[2 * t].astype(F32), pre_ref[2 * t + 1].astype(F32)], axis=1)
        pre2[t] = both.astype(BF)

    col = lax.broadcasted_iota(jnp.int32, (C, C // 2), 1)
    row = lax.broadcasted_iota(jnp.int32, (C, C // 2), 0)
    pick = jnp.where(row == 64 * (col // 32) + 32 * c + col % 32, 1.0, 0.0).astype(BF)
    wi_own[...] = jnp.dot(wi_ref[...], pick, preferred_element_type=F32).astype(BF)

    near = [take_block(dz) for dz in steps]
    pass_cells(0)
    pass_cells(1)

    @pl.when(across)
    def _():
        take_block(0)

    near.append(z)
    go_copy.wait_recv()
    project(stack(near), near, 0)
    for n in range(2, NF):
        pass_cells(n)
    handed = go_buf.at[pl.ds(0, 128), :]
    remote(handed, handed, gf_s.at[0], gf_r.at[0], d, partner).wait_recv()
    project(stack(near), near, 1)
    ring_i.begin()
    if Z >= 8:
        distant = [take_block(dz) for dz in (3, -3, 4)]
        rows = stack(distant)
        project(rows, distant, 0)
        project(rows, distant, 1)
    up, down = jnp.minimum(d + 1, DN - 1), jnp.maximum(d - 1, 0)

    def halo(n, side):
        part = pl.ds(1 + 2 * KPC * n, 2 * KPC)
        return remote(
            m_buf.at[1, part],
            m_buf.at[2 if side == 0 else 0, part],
            h_s.at[side],
            h_r.at[side, n],
            up if side == 0 else down,
            h,
        )

    turn = [(k // KPC + j) % NCH for j in range(NCH)]
    for j, n in enumerate(turn):
        tiles = 2 * KPC - 2 * (j == 0) - 2 * (j == NCH // 2)
        part = m_buf.at[1, pl.ds(1, tiles)]
        remote(part, part, a1_s.at[0], a1_r.at[n], d, partner).wait_recv()

        @pl.when(d < DN - 1)
        def _(n=n):
            halo(n, 0).start()

        @pl.when(d > 0)
        def _(n=n):
            halo(n, 1).start()

    lane = lax.broadcasted_iota(jnp.int32, (5, 32, 128), 2)
    low = lane < 64
    first = lane % 64 == 0
    last = lane % 64 == 63

    def shifts(v):
        n = v.shape[0]
        zero = jnp.zeros_like(v)
        later = jnp.where(last[:n], zero, pltpu.roll(v, 127, 2))
        sooner = jnp.where(first[:n], zero, pltpu.roll(v, 1, 2))
        return later, v, sooner

    def columns(s, q):
        tiles = m_buf[s, pl.ds(4 * q, 6)]
        half = pltpu.roll(tiles, 64, 2)
        even = shifts(tiles[1:5])
        odd = shifts(jnp.where(low, half[0:5], half[1:6]))
        parts = []
        for j in range(4):
            column = [v[j + 1] for v in odd] + [v[j] for v in even] + [v[j] for v in odd]
            parts.append(jnp.concatenate(column, axis=0))
        return jnp.concatenate(parts, axis=1)

    def hidden(q):
        tiles = [jnp.maximum(pre2[4 * q + j], jnp.zeros((32, 128), BF)) for j in range(4)]
        return jnp.concatenate(tiles, axis=1)

    def outer(x, q):
        return lax.dot_general(hidden(q), x, (((1,), (1,)), ((), ())), preferred_element_type=F32)

    gbuf[...] = jnp.zeros_like(gbuf)

    @pl.loop(0, NQ, unroll=min(NQ, 8))
    def _(q):
        x = columns(1, q)
        acc[q] = jnp.dot(kmat[1], x, preferred_element_type=F32)
        gbuf[1, :, 0:288] += outer(x, q)

    def finish_quads(quads):
        for q in quads:
            back = acc[q]
            for s in (0, 2):
                x = columns(s, q)
                back = back + jnp.dot(kmat[s], x, preferred_element_type=F32)
                gbuf[s, :, 0:288] += outer(x, q)
            for j in range(4):
                gate = pre2[4 * q + j].astype(F32) > 0
                tile = jnp.where(gate, back[:, 128 * j : 128 * j + 128], jnp.zeros((32, 128), F32))
                gp_stage[4 * q + j] = tile.astype(BF)
        for q in quads:
            for j in range(2):
                i = 2 * q + j

                @pl.when(i == k)
                def _(i=i):
                    for t in range(2):
                        gpr[t, pl.ds(pl.multiple_of(32 * k, 32), 32), :] = gp_stage[2 * i + t]

                @pl.when(i != k)
                def _(i=i):
                    remote(
                        gp_stage.at[pl.ds(2 * i, 2)],
                        gpr.at[:, pl.ds(pl.multiple_of(32 * k, 32), 32), :],
                        a2_s.at[0],
                        a2_r.at[0],
                        d,
                        2 * i + c,
                    ).start()

    done = 0
    for j, n in enumerate(turn):
        @pl.when(d < DN - 1)
        def _(n=n):
            halo(n, 1).wait_recv()

        @pl.when(d > 0)
        def _(n=n):
            halo(n, 0).wait_recv()

        ratio = NQ // NCH
        ready = NQ if j == NCH - 1 else max(0, j * ratio - (ratio == 1))
        while done < ready:
            finish_quads([(turn[0] * (NQ // NCH) + 1 + p) % NQ for p in range(done, min(done + 2, ready))])
            done = min(done + 2, ready)
        if j == NCH // 2:
            for far, dz in ring_i.first:
                ring_i.take(far, dz)
                ring_i.share(far, dz)

    def slot(f):
        return f // SPD, f % SPD

    def cut(f):
        s, rest = divmod(f, 12)
        rb, lt = divmod(rest, 3)
        return s, slice(8 * rb, 8 * rb + 8), slice(128 * lt, 128 * lt + 128)

    for f in range(SPD * DN):
        a, b = slot(f)
        g_stage[a, b] = gbuf[cut(f)].astype(BF) if f < 36 else jnp.zeros((8, 128), BF)

    @pl.loop(1, DN)
    def _(j):
        r = (d + j) % DN
        remote(g_stage.at[r], g_recv.at[d], rs_s.at[0], rs_r.at[0], r, h).start()

    for far, dz in ring_i.second:
        ring_i.take(far, dz)
        ring_i.share(far, dz)

    part = g_recv.at[pl.ds(0, DN - 1)]
    remote(part, part, rs_s.at[0], rs_r.at[0], d, partner).wait_recv()
    total = g_stage[d].astype(F32)
    for j in range(1, DN):
        r = (d + j) % DN
        total = total + g_recv[r].astype(F32)
    g_fin[d] = total.astype(BF)

    @pl.loop(1, DN)
    def _(j):
        r = (d + j) % DN
        remote(g_fin.at[d], g_fin.at[d], ag_s.at[0], ag_r.at[0], r, h).start()

    part = wi_buf.at[pl.ds(0, DN - 1), pl.ds(0, 32), :]
    remote(part, part, wi_s.at[0], wi_rest.at[0], d, partner).wait_recv()
    wi_buf[d] = wi_own[...]

    part = gpr.at[:, pl.ds(0, 32 * (DN - 1)), :]
    remote(part, part, a2_s.at[0], a2_r.at[0], d, partner).wait_recv()

    rows_p = wi_buf.shape[0] // NP

    def half(cells, n):
        w = wi_buf[rows_p * n : rows_p * (n + 1)].reshape(PW, C // 2)
        return lax.dot_general(cells, w, (((1,), (1,)), ((), ())), preferred_element_type=F32)

    theirs = gpr[1 - c].T
    exchange = []
    for n in range(NP):
        p_send[n] = half(theirs, n)
        copy = remote(p_send.at[n], p_recv.at[n], p_s.at[0], p_r.at[n], d, partner)
        copy.start()
        exchange.append(copy)

    mine = gpr[c].T
    for n in range(NP):
        part = half(mine, n)
        exchange[n].wait_recv()
        cols = slice(PW * n, PW * (n + 1))
        out_ref[:, cols] = (go_buf[own_cells, cols].astype(F32) + (part + p_recv[n])).astype(BF)

    part = g_fin.at[pl.ds(0, DN - 1)]
    remote(part, part, ag_s.at[0], ag_r.at[0], d, partner).wait_recv()

    scale = float(DN * 2 * HN * 64) ** -0.5
    for f in range(36):
        gbuf[cut(f)] = g_fin[slot(f)].astype(F32) * scale
    for o in range(27):
        s, m = divmod(o, 9)
        kg_ref[o] = gbuf[s, :, 32 * m : 32 * m + 32]


    go_copy.wait_send()
    for there, blocks in ((xh == xl, Z - 1), (across, Z)):
        @pl.when(there)
        def _(blocks=blocks):
            sent = wo_buf.at[pl.ds(0, blocks)]
            remote(sent, sent, wo_s.at[0], wo_r.at[0], d, partner).wait_send()

    ring_i.finish()

    def left(part, sem):
        remote(part, part, sem, go_sem.at[1], d, partner).wait_send()

    left(p_send, p_s.at[0])
    for side, there in ((0, d < DN - 1), (1, d > 0)):
        @pl.when(there)
        def _(side=side):
            left(m_buf.at[1, pl.ds(1, HN)], h_s.at[side])

    left(mt_buf.at[pl.ds(0, DN - 2)], a1_s.at[0])
    left(go_buf.at[pl.ds(0, 128), :], gx_s.at[0])
    left(go_buf.at[pl.ds(0, 128), :], gf_s.at[0])
    left(gp_stage.at[pl.ds(0, 2 * (DN - 1))], a2_s.at[0])
    left(g_stage.at[pl.ds(0, DN - 1)], rs_s.at[0])
    left(g_fin.at[pl.ds(0, DN - 1)], ag_s.at[0])


def shards(DN, grad_out, pre_act, w_in, w_out, kernel):
    C = grad_out.shape[-1]
    HN = 2 * DN
    rows = grad_out.reshape(128, C)
    turned = jnp.transpose(pre_act, (0, 1, 3, 2)).reshape(2 * HN, 32, 64)
    nch = DN // 2
    spd = -(-36 // DN)
    np_ = max(1, C // 256)
    dma = pltpu.SemaphoreType.DMA
    grad_in, kernel_grad = pl.pallas_call(
        functools.partial(body, DN, C),
        out_shape=(
            pltpu.VMEM((128, C), BF),
            pltpu.VMEM((27, 32, 32), F32),
        ),
        in_specs=[pl.BlockSpec(memory_space=pltpu.HBM)] * 5,
        out_specs=(pl.BlockSpec(memory_space=pltpu.VMEM),) * 2,
        scratch_shapes=[
            pltpu.VMEM((2 * HN, 32, 64), BF),
            pltpu.VMEM((64, C), BF),
            pltpu.VMEM((32, C), BF),
            pltpu.VMEM((27, 32, 32), BF),
            pltpu.VMEM((512, C), BF),
            pltpu.VMEM((DN // 2, 32, C), BF),
            pltpu.VMEM((DN, 64, C // 2), BF),
            pltpu.VMEM((64, C // 2), BF),
            pltpu.VMEM((DN, 2, 32, 128), BF),
            pltpu.VMEM((3, HN + 2, 32, 128), BF),
            pltpu.VMEM((HN, 32, 128), BF),
            pltpu.VMEM((3, 32, 288), F32),
            pltpu.VMEM((3, 32, 288), BF),
            pltpu.VMEM((HN // 4, 32, 512), F32),
            pltpu.VMEM((HN, 32, 128), BF),
            pltpu.VMEM((2, C // 2, 128), BF),
            pltpu.VMEM((3, 32, 384), F32),
            pltpu.VMEM((DN, spd, 8, 128), BF),
            pltpu.VMEM((DN, spd, 8, 128), BF),
            pltpu.VMEM((DN, spd, 8, 128), BF),
            pltpu.VMEM((np_, 128, C // np_), F32),
            pltpu.VMEM((np_, 128, C // np_), F32),
            dma((5,)),
            dma((2,)),
            dma((1,)),
            dma((4,)),
            dma((1,)),
            dma((1,)),
            dma((1,)),
            dma((DN // 2,)),
            dma((1,)),
            dma((1, DN)),
            dma((1,)),
            dma((1,)),
            dma((nch,)),
            dma((2,)),
            dma((2, nch)),
            dma((1,)),
            dma((1,)),
            dma((1,)),
            dma((1,)),
            dma((1,)),
            dma((1,)),
            dma((1,)),
            dma((np_,)),
        ],
        compiler_params=pltpu.CompilerParams(
            collective_id=0, has_side_effects=True, vmem_limit_bytes=63 << 20
        ),
    )(rows, turned, w_in, w_out, kernel)
    return grad_in.reshape(grad_out.shape), kernel_grad


def solution(mesh):
    in_specs = (
        P("depth", "height", None, None),
        P("depth", None, None, "height"),
        P("depth", None),
        P("depth", None),
        P(None, None, "height"),
    )
    out_specs = (P("depth", "height", None, None), P(None, None, "height"))
    step = functools.partial(shards, mesh.shape["depth"])
    return jax.shard_map(step, mesh=mesh, in_specs=in_specs, out_specs=out_specs, check_vma=False)
```
